256 devices in a mesh: lon: 32 (over x, z_hi, core), lat: 8 (over z_lo, y).
Axes of the slice: x: 4, y: 4, z: 8 (z_hi: 4, z_lo: 2; z = z_hi * 2 + z_lo), core: 2. Of those that a mesh axis runs over, the one named last changes fastest.
Arguments:
- cotangent: bfloat16 [256, 128, 512], P('lon', 'lat'), may hold values from -6 to 6
- states: bfloat16 [3, 256, 128, 512], P(None, 'lon', 'lat'), may hold values from -6 to 6
- w_up: bfloat16 [512, 1024], replicated, may hold values from -0.25 to 0.25
- w_down: bfloat16 [512, 1024], replicated, may hold values from -0.1875 to 0.1875
- norm_gain: float32 [512], replicated, may hold values from 0.5 to 1.5
- kernel: float32 [3, 3, 512], replicated, may hold values from -0.6 to 0.6
- bilinear: float32 [3, 4, 256, 128], P(None, None, 'lon', 'lat'), may hold values from 0.05 to 0.5
- lon_move: int32 [3, 4], replicated, may hold values from 0 to 63, as said below
- lat_move: int32 [3, 4], replicated, may hold values from 0 to 31
Outputs:
- grad_state: bfloat16 [256, 128, 512], P('lon', 'lat')
- grad_up: float32 [512, 1024], P('lon', 'lat')
- grad_down: float32 [512, 1024], P('lon', 'lat')
- grad_kernel: float32 [3, 3, 512], replicated
- grad_gain: float32 [512], replicated
The draws below stay inside these ranges and needn't reach their ends.
Inputs may be any that keep to these rules, and one draw needn't show every extreme that they name: `lon_move`: a whole number of longitude tiles below 8, times 8, plus an offset below 8.
All inputs are finite; a program needn't handle non-finite values.
Results may differ from the reference program's by a relative error of at most 0.02.
Values may be sent and summed in bfloat16 or wider, within the bound.
A program may use at most 64 MiB of HBM per device.

```python
import jax
import jax.numpy as jnp
from jax import lax

GROUP = 128
GROUPS = 4
HID = 1024
STEPS = 3
REACH = 8
CLON = 8
CLAT = 16
C = 512
NLON = 256
NLAT = 128


def draw_lon_move(key, part):
    tile_steps = jax.random.randint(jax.random.fold_in(key, 11), (STEPS, GROUPS), 0, REACH)
    levels = REACH.bit_length() - 1
    forced = jnp.array([1 << group_index % levels for group_index in range(GROUPS)], jnp.int32)
    tile_steps = jnp.bitwise_or(tile_steps, forced[None, :])
    offsets = jax.random.randint(jax.random.fold_in(key, 12), (STEPS, GROUPS), 0, CLON)
    return (tile_steps * CLON + offsets).astype(jnp.int32)


def draw_lat_move(key, part):
    upper_tile = jax.random.randint(jax.random.fold_in(key, 21), (STEPS, GROUPS), 0, 2)
    step_iota = lax.broadcasted_iota(jnp.int32, (STEPS, GROUPS), 0)
    group_iota = lax.broadcasted_iota(jnp.int32, (STEPS, GROUPS), 1)
    upper_tile = jnp.where(group_iota == step_iota % GROUPS, 1, upper_tile)
    offsets = jax.random.randint(jax.random.fold_in(key, 22), (STEPS, GROUPS), 0, CLAT)
    return (upper_tile * CLAT + offsets).astype(jnp.int32)


def block_levels(key, shape, cuts, least, top_value):
    loudness, own = 1.0, jax.random.fold_in(key, 6)
    for axis_at, shards_of in cuts:
        draws = jnp.exp(jax.random.uniform(jax.random.fold_in(own, axis_at), (shards_of,), jnp.float32, least / len(cuts), top_value / len(cuts)))
        loudness = loudness * jnp.repeat(draws, shape[axis_at] // shards_of).reshape([-1 if axis == axis_at else 1 for axis in range(len(shape))])
    return loudness


def gaussian(key, extent, deviation, limit, split=(), held_as=jnp.bfloat16):
    entries = jax.random.normal(key, extent, jnp.float32) * deviation
    if len(split) > 0:
        entries = block_levels(key, extent, split, -0.22, 0.18) * entries
    return jnp.clip(entries, min=-limit, max=limit).astype(held_as)


def setup_inputs(seed: int = 0) -> dict:
    key_list = jax.random.split(jax.random.key(seed), 10)
    return {
        "cotangent": gaussian(key_list[0], (NLON, NLAT, C), 1.0, 6.0, ((0, 32), (1, 8))),
        "states": gaussian(key_list[1], (STEPS, NLON, NLAT, C), 1.0, 6.0, ((1, 32), (2, 8))),
        "w_up": gaussian(key_list[2], (C, HID), C ** -0.5, 0.25),
        "w_down": gaussian(key_list[3], (C, HID), HID ** -0.5, 0.1875),
        "norm_gain": jnp.clip(1.0 + 0.1 * jax.random.normal(key_list[4], (C,), jnp.float32), 0.5, 1.5),
        "kernel": gaussian(key_list[5], (3, 3, C), 0.15, 0.6, (), jnp.float32),
        "bilinear": jnp.clip(0.05 + 0.45 * jax.random.uniform(key_list[6], (STEPS, 4, NLON, NLAT), jnp.float32) ** block_levels(key_list[6], (STEPS, 4, NLON, NLAT), ((2, 32), (3, 8)), -0.2, 0.2), 0.05, 0.5),
        "lon_move": draw_lon_move(jax.random.fold_in(key_list[9], 71), 0),
        "lat_move": draw_lat_move(jax.random.fold_in(key_list[9], 71), 0),
    }


EPSILON = 1e-06

def widen_field(field):
    beside_all = jnp.concatenate([field[-1:], field, field[:1]], axis=0)
    return jnp.pad(beside_all, ((0, 0), (1, 1), (0, 0)))

def tapped(padded, kernel, rows_out, cols_out, mirror):
    running = jnp.zeros((rows_out, cols_out, padded.shape[2]), jnp.float32)
    for row_tap in range(3):
        for col_tap in range(3):
            start_row = 2 - row_tap if mirror else row_tap
            start_col = 2 - col_tap if mirror else col_tap
            window = padded[start_row:start_row + rows_out, start_col:start_col + cols_out].astype(jnp.float32)
            running = running + kernel[row_tap, col_tap] * window
    return running

def next_lat(values):
    return jnp.concatenate([values[:, 1:], jnp.zeros_like(values[:, :1])], axis=1)

def step_back(state_now, upstream, w_up, w_down, norm_gain, kernel, weights_now, lon_now, lat_now):
    rows_out, cols_out, channels = state_now.shape
    padded_state = widen_field(state_now)
    mixed_field = state_now.astype(jnp.float32) + tapped(padded_state, kernel, rows_out, cols_out, False)
    inv_root = lax.rsqrt(lax.optimization_barrier(jnp.mean(mixed_field * mixed_field, axis=-1, keepdims=True)) + EPSILON)
    normed = mixed_field * inv_root
    normed_rows = (normed * norm_gain).astype(jnp.bfloat16).reshape(-1, channels)
    hidden_pre = jnp.dot(normed_rows, w_up, preferred_element_type=jnp.float32)
    hidden = jax.nn.silu(hidden_pre).astype(jnp.bfloat16)
    upstream_f = upstream.astype(jnp.float32)
    weighted = [weights_now[corner][:, :, None] * upstream_f for corner in range(4)]
    spread = weighted[0] + jnp.roll(weighted[1], -1, axis=0) + next_lat(weighted[2])
    spread = spread + next_lat(jnp.roll(weighted[3], -1, axis=0))
    spread = spread.astype(jnp.bfloat16)
    pieces = []
    for group_index in range(GROUPS):
        group_piece = spread[:, :, group_index * GROUP:(group_index + 1) * GROUP]
        group_piece = jnp.roll(group_piece, -lon_now[group_index], axis=0)
        padded = jnp.concatenate([group_piece, jnp.zeros_like(group_piece)], axis=1)
        pieces.append(lax.dynamic_slice_in_dim(padded, lat_now[group_index], cols_out, 1))
    moved_back = jnp.concatenate(pieces, axis=2)
    moved_rows = moved_back.reshape(-1, channels)
    grad_hidden = jnp.dot(moved_rows, w_down, preferred_element_type=jnp.float32)
    sigmoid_pre = jax.nn.sigmoid(hidden_pre)
    grad_pre = (grad_hidden * sigmoid_pre * (1.0 + hidden_pre * (1.0 - sigmoid_pre))).astype(jnp.bfloat16)
    grad_normed = lax.dot_general(grad_pre, w_up, (((1,), (1,)), ((), ())), preferred_element_type=jnp.float32)
    grad_normed = grad_normed.reshape(rows_out, cols_out, channels)
    lead_contract = (((0,), (0,)), ((), ()))
    term_up = lax.dot_general(normed_rows, grad_pre, lead_contract, preferred_element_type=jnp.float32)
    term_down = lax.dot_general(moved_rows, hidden, lead_contract, preferred_element_type=jnp.float32)
    term_gain = lax.optimization_barrier(jnp.sum(grad_normed * normed, axis=(0, 1)))
    scaled = grad_normed * norm_gain
    grad_mixed = inv_root * (scaled - normed * lax.optimization_barrier(jnp.mean(scaled * normed, axis=-1, keepdims=True)))
    grad_field = (moved_back.astype(jnp.float32) + grad_mixed).astype(jnp.bfloat16)
    padded_grad = widen_field(grad_field)
    result = grad_field.astype(jnp.float32) + tapped(padded_grad, kernel, rows_out, cols_out, True)
    grad_f = grad_field.astype(jnp.float32)
    term_kernel = jnp.stack([jnp.stack([lax.optimization_barrier(jnp.sum(padded_state[row_tap:row_tap + rows_out, col_tap:col_tap + cols_out].astype(jnp.float32) * grad_f, axis=(0, 1))) for col_tap in range(3)]) for row_tap in range(3)])
    return (result.astype(jnp.bfloat16), term_up, term_down, term_kernel, term_gain)

def reference(cotangent, states, w_up, w_down, norm_gain, kernel, bilinear, lon_move, lat_move):
    upstream = cotangent
    acc_up = jnp.zeros(w_up.shape, jnp.float32)
    acc_down = jnp.zeros(w_down.shape, jnp.float32)
    acc_kernel = jnp.zeros(kernel.shape, jnp.float32)
    acc_gain = jnp.zeros(norm_gain.shape, jnp.float32)
    for index_step in reversed(range(STEPS)):
        upstream, term_up, term_down, term_kernel, term_gain = step_back(states[index_step], upstream, w_up, w_down, norm_gain, kernel, bilinear[index_step], lon_move[index_step], lat_move[index_step])
        acc_up = acc_up + term_up
        acc_down = acc_down + term_down
        acc_kernel = acc_kernel + term_kernel
        acc_gain = acc_gain + term_gain
    return (upstream, acc_up, acc_down, acc_kernel, acc_gain)
```

```python
import jax
import jax.numpy as jnp
from jax import lax
from jax.experimental import pallas as pl
from jax.experimental.pallas import tpu as pltpu
from jax.sharding import PartitionSpec as P

GROUPS = 4
STEPS = 3
EPSILON = 1e-06
MESH = pl.DeviceIdType.MESH
F32 = jnp.float32
BF16 = jnp.bfloat16

NX, NZH, NZL, NY = 4, 4, 2, 4
LON, LAT = NX * NZH * 2, NZL * NY
AHEAD = 4
PW = 32
GW = 24


def kernel(
    cot, st, wu, wd, gain, kern, bt, lm, lt,
    gs_out, up_out, dn_out, kern_out, gain_out,
    px, pf, gg, wb, pt, fld, stg, hb, sxs, sxr, br1, br2, br3,
    win, near_by, ps, pr, lon2, lb, lw, lwin, diff,
    mv, nn, hid, ds, nrm, inv, gp, gn, accu, accd, kacc, gacc,
    cs, cr, b1u, ryu, b2u, rxu, b3u, rzu, b1d, rxd, b2d, ryd, b3d, rzd,
    smc, smy, smx, smz,
    s_sx, r_sx, s_bt, r_bt, s_h, r_h, s_l, r_l, s_p, r_p, s_t, r_t,
    s_c, r_c, s_y, r_y, s_x, r_x, s_z, r_z, s_sm, r_sm,
):
    lon = lax.axis_index("lon")
    lat = lax.axis_index("lat")
    core = lax.rem(lon, 2)
    chip = lon // 2
    xx, zh = chip // NZH, lax.rem(chip, NZH)
    zl, yy = lat // NY, lax.rem(lat, NY)
    mate = lon + 1 - 2 * core

    def at(dlon, dlat):
        return (lax.rem(lon + dlon + LON, LON), lax.rem(lat + dlat + LAT, LAT))

    def at_y(d):
        return (lon, zl * NY + lax.rem(yy + d, NY))

    def at_x(d):
        return (lax.rem(xx + d, NX) * (2 * NZH) + zh * 2 + core, lat)

    def at_z(dzl, dzh):
        return (
            (xx * NZH + lax.rem(zh + dzh, NZH)) * 2 + core,
            lax.rem(zl + dzl, NZL) * NY + yy,
        )

    def send(src, dst, ssem, rsem, target):
        pltpu.make_async_remote_copy(
            src_ref=src, dst_ref=dst, send_sem=ssem, recv_sem=rsem,
            device_id=target, device_id_type=MESH,
        ).start()

    def drain(ref, sem):
        pltpu.make_async_copy(ref, ref, sem).wait()

    near = [(a, b) for a in (-1, 0, 1) for b in (-1, 0, 1) if (a, b) != (0, 0)]
    zpairs = [(a, b) for a in range(NZL) for b in range(NZH) if (a, b) != (0, 0)]
    partners = [at(a, b) for a, b in near]
    partners += [at(2 * d * sign, 0) for d in range(1, AHEAD + 1) for sign in (-1, 1)]
    partners += [at(0, 2), at(0, -2)]
    partners += [at_y(d) for d in range(1, NY)] + [at_x(d) for d in range(1, NX)]
    partners += [at_z(a, b) for a, b in zpairs]
    barrier = pltpu.get_barrier_semaphore()
    for target in partners:
        pl.semaphore_signal(barrier, inc=1, device_id=target, device_id_type=MESH)

    def column(ref, j):
        return [ref[i, j : j + 1] for i in range(1, 9)]

    def put_column(ref, j, rows):
        for i in range(8):
            ref[i + 1, j : j + 1] = rows[i : i + 1]

    not_low = lat > 0
    not_high = lat < LAT - 1
    for i in range(8):
        block = cot[i]
        fld[0, i] = block
        pf[i + 1, 8:24] = block.astype(F32)
        for s in range(STEPS):
            px[s, i + 1, 8:24] = st[s, i].astype(F32)
    for s in range(STEPS):
        sxs[s] = jnp.concatenate(
            column(px.at[s], 8) + column(px.at[s], 23), axis=0
        ).astype(BF16)
    place = lax.broadcasted_iota(jnp.int32, diff.shape, 0)
    diff[...] = (
        lax.broadcasted_iota(jnp.int32, diff.shape, 1)
        - lax.div(place, 16) * 48 - lax.rem(place, 16)
    )
    pl.semaphore_wait(barrier, len(partners))

    def halo_send(it):
        first, second, last = column(pf, 8), column(pf, 9), column(pf, 23)
        stg[it, 0] = jnp.concatenate(first + second, axis=0).astype(BF16)
        stg[it, 1] = jnp.concatenate(last + last, axis=0).astype(BF16)
        low, high = stg.at[it, 0], stg.at[it, 1]

        def go(src, block, target, k):
            send(src, hb.at[it, block], s_h.at[it, k], r_h.at[it], target)

        send(fld.at[it, 0:2], hb.at[it, 1:3], s_h.at[it, 1], r_h.at[it], at(-1, 0))
        go(fld.at[it, 7], 0, at(1, 0), 0)
        go(high, 3, at(0, 1), 2)
        go(low, 4, at(0, -1), 3)
        go(high, 5, at(1, 1), 4)
        go(low, 6, at(1, -1), 5)
        go(high, 7, at(-1, 1), 6)
        go(low, 8, at(-1, -1), 7)

    def halo_sent(it):
        drain(fld.at[it, 7], s_h.at[it, 0])
        drain(fld.at[it, 0:2], s_h.at[it, 1])
        for k in range(2, 8):
            drain(stg.at[it, 0], s_h.at[it, k])

    def cut(keep, value):
        return jnp.where(keep, value, jnp.zeros_like(value))

    def halo_fill(it):
        drain(hb.at[it], r_h.at[it])
        block = [hb[it, k].astype(F32) for k in range(9)]
        pf[0, 8:24] = block[0]
        pf[9, 8:24] = block[1]
        pf[10, 8:24] = block[2]
        lo, hi = cut(not_low, block[3]), cut(not_high, block[4])
        put_column(pf, 7, lo[8:16])
        put_column(pf, 24, hi[0:8])
        put_column(pf, 25, hi[8:16])
        lo, hi = cut(not_low, block[5]), cut(not_high, block[6])
        pf[0, 7:8] = lo[15:16]
        pf[0, 24:25] = hi[7:8]
        pf[0, 25:26] = hi[15:16]
        lo, hi = cut(not_low, block[7]), cut(not_high, block[8])
        for r in (9, 10):
            pf[r, 7:8] = lo[8 + r - 9 : 8 + r - 8]
            pf[r, 24:25] = hi[r - 9 : r - 8]
            pf[r, 25:26] = hi[8 + r - 9 : 8 + r - 8]

    def stencil(it, rows):
        on = jnp.where(it > 0, 1.0, 0.0).astype(F32)

        def row(i, carry):
            for k in range(GROUPS):
                lanes = pl.ds(128 * k, 128)
                total = pf[i + 1, 8 : 6 + GW, lanes]
                centre = total
                running = jnp.zeros_like(total)
                for a in range(3):
                    for b in range(3):
                        tap = kern[pl.ds(3 * a + b, 1), lanes] * on
                        running = running + tap * (
                            pf[i + 2 - a, 9 - b : 9 - b + GW - 2, lanes]
                        )
                gg[i, 0 : GW - 2, lanes] = (centre + running).astype(BF16).astype(F32)
            return carry

        lax.fori_loop(0, rows, row, 0)

    def accumulate(s):
        def block(j, carry):
            pair = jnp.concatenate([gp[2 * j], gp[2 * j + 1]], axis=1)
            part = lax.dot_general(
                nn[...], pair, (((0,), (0,)), ((), ())), preferred_element_type=F32
            )
            accu[2 * j] += part[:, :128].reshape(16, 2, 16, 128)
            accu[2 * j + 1] += part[:, 128:].reshape(16, 2, 16, 128)
            pair = jnp.concatenate([hid[2 * j], hid[2 * j + 1]], axis=1)
            part = lax.dot_general(
                mv[...], pair, (((0,), (0,)), ((), ())), preferred_element_type=F32
            )
            accd[2 * j] += part[:, :128].reshape(16, 2, 16, 128)
            accd[2 * j + 1] += part[:, 128:].reshape(16, 2, 16, 128)
            return carry

        lax.fori_loop(0, 4, block, 0)

        def row(i, carry):
            f = pf[i + 1, 8:24]
            for a in range(3):
                for b in range(3):
                    prod = px[s, i + a, 7 + b : 23 + b] * f
                    kacc[3 * a + b] += prod[:8] + prod[8:]
            rows = pl.ds(pl.multiple_of(i * 16, 16), 16)
            prod = gn[rows, :] * nrm[rows, :]
            gacc[...] += prod[:8] + prod[8:]
            return carry

        lax.fori_loop(0, 8, row, 0)

    def spread(it, s):
        for k in range(GROUPS):
            lanes = pl.ds(128 * k, 128)

            def row(i, carry):
                own = wb[s, 0, i] * gg[i, 0:16, lanes]
                own = own + wb[s, 1, i] * gg[i + 1, 0:16, lanes]
                own = own + wb[s, 2, i] * gg[i, 1:17, lanes]
                own = own + wb[s, 3, i] * gg[i + 1, 1:17, lanes]
                win[it, k, 0, i] = own.astype(BF16)
                return carry

            lax.fori_loop(0, 8, row, 0)
            for d in range(1, AHEAD + 1):
                send(
                    win.at[it, k, 0], win.at[it, k, d], s_l.at[it, k], r_l.at[it, k],
                    at(-2 * d, 0),
                )

    def forward(s):
        def row(i, carry):
            u = px[s, i + 1, 8:24]
            running = jnp.zeros_like(u)
            for a in range(3):
                for b in range(3):
                    running = running + kern[pl.ds(3 * a + b, 1), :] * (
                        px[s, i + a, 7 + b : 23 + b]
                    )
            u = u + running
            root = lax.rsqrt(jnp.mean(u * u, axis=-1, keepdims=True) + EPSILON)
            rows = pl.ds(pl.multiple_of(i * 16, 16), 16)
            normed = u * root
            nrm[rows, :] = normed
            inv[rows, :] = jnp.broadcast_to(root, (16, 128))
            nn[rows, :] = (normed * gain[...]).astype(BF16)
            return carry

        lax.fori_loop(0, 8, row, 0)

        def block(j, carry):
            cols = pl.ds(pl.multiple_of(j * 256, 256), 256)
            pre = jnp.dot(nn[...], wu[:, cols], preferred_element_type=F32)
            sig = jax.nn.sigmoid(pre)
            hidden = (pre * sig).astype(BF16)
            slope = sig * (1.0 + pre * (1.0 - sig))
            for h in range(2):
                hid[2 * j + h] = hidden[:, 128 * h : 128 * (h + 1)]
                ds[2 * j + h] = slope[:, 128 * h : 128 * (h + 1)]
            return carry

        lax.fori_loop(0, 4, block, 0)

    def transport(it, s):
        for k in range(GROUPS + 2):
            if k < GROUPS:
                g = k
                drain(win.at[it, g, 1 : AHEAD + 1], r_l.at[it, g])
                for d in range(AHEAD + 1):
                    near_by[g, d] = win[it, g, d]
                far = lax.div(lm[s, g], 8)
                ps[it, g] = near_by[g, lax.div(far, 2) + 1 - core]
                send(ps.at[it, g], pr.at[it, g], s_p.at[it, g], r_p.at[it, g], (mate, lat))
            if 1 <= k <= GROUPS:
                g = k - 1
                drain(pr.at[it, g], r_p.at[it, g])
                move = lm[s, g]
                far = lax.div(move, 8)
                odd = pr[it, g]
                lon2[g, 0:8] = odd
                lon2[g, 8:16] = near_by[g, lax.div(far + 1, 2)]
                lon2[g, 16:24] = odd
                begin = 8 - 8 * lax.rem(far, 2) + lax.rem(move, 8)
                for i in range(8):
                    own = lon2[g, begin + i]
                    lb[it, g, i] = own
                    lwin[g, i, 0:16] = own
                for d in (1, 2):
                    send(
                        lb.at[it, g], lw.at[it, g, d - 1], s_t.at[it, g], r_t.at[it, g],
                        at(0, -d),
                    )
            if k >= 2:
                g = k - 2
                drain(lw.at[it, g], r_t.at[it, g])
                lwin[g, :, 16:32] = cut(lat < LAT - 1, lw[it, g, 0])
                lwin[g, :, 32:48] = cut(lat < LAT - 2, lw[it, g, 1])
                pick = jnp.where(diff[...] == lt[s, g], 1.0, 0.0).astype(BF16)
                mv[:, 128 * g : 128 * (g + 1)] = jnp.dot(
                    pick, lwin[g].reshape(8 * 48, 128), preferred_element_type=F32
                ).astype(BF16)

    def backward(it):
        total = None
        for j in range(4):
            cols = slice(256 * j, 256 * (j + 1))
            up = jnp.dot(mv[...], wd[:, cols], preferred_element_type=F32)
            slope = jnp.concatenate([ds[2 * j], ds[2 * j + 1]], axis=1)
            pre = (up * slope).astype(BF16)
            gp[2 * j] = pre[:, :128]
            gp[2 * j + 1] = pre[:, 128:]
            part = lax.dot_general(
                pre, wu[:, cols], (((1,), (1,)), ((), ())), preferred_element_type=F32
            )
            total = part if total is None else total + part
        gn[...] = total

        def row(i, carry):
            rows = pl.ds(pl.multiple_of(i * 16, 16), 16)
            normed = nrm[rows, :]
            scaled = gn[rows, :] * gain[...]
            mean = jnp.mean(scaled * normed, axis=-1, keepdims=True)
            root = jnp.concatenate([inv[rows, :]] * GROUPS, axis=1)
            field = (mv[rows, :].astype(F32) + root * (scaled - normed * mean)).astype(BF16)
            fld[it + 1, i] = field
            pf[i + 1, 8:24] = field.astype(F32)
            return carry

        lax.fori_loop(0, 8, row, 0)

    halo_send(0)
    send(bt.at[0:16], br1, s_bt.at[0], r_bt.at[0], at(-1, 0))
    send(bt, br2, s_bt.at[1], r_bt.at[1], at(0, -1))
    send(bt.at[0:8], br3, s_bt.at[2], r_bt.at[2], at(-1, -1))
    state_edges = [
        (st.at[:, 7], at(1, 0)), (st.at[:, 0], at(-1, 0)), (sxs, at(0, 1)), (sxs, at(0, -1)),
        (sxs, at(1, 1)), (sxs, at(1, -1)), (sxs, at(-1, 1)), (sxs, at(-1, -1)),
    ]
    for k, (src, target) in enumerate(state_edges):
        send(src, sxr.at[k], s_sx.at[k], r_sx, target)

    accu[...] = jnp.zeros_like(accu)
    accd[...] = jnp.zeros_like(accd)
    kacc[...] = jnp.zeros_like(kacc)
    gacc[...] = jnp.zeros_like(gacc)

    for i in range(8):
        pt[i, 0:16] = bt[pl.ds(i * 16, 16), :]
    drain(br1, r_bt.at[0])
    drain(br2, r_bt.at[1])
    drain(br3, r_bt.at[2])
    pt[8, 0:16] = br1[...]
    for i in range(8):
        pt[i, 16:17] = cut(not_high, br2[pl.ds(16 * i, 1), :])
    pt[8, 16:17] = cut(not_high, br3[pl.ds(0, 1), :])

    def weights(i, carry):
        for q, (di, dj) in enumerate(((0, 0), (1, 0), (0, 1), (1, 1))):
            rows = pt[i + di, dj : dj + 16]
            for s in range(STEPS):
                lane = 4 * s + q
                wb[s, q, i] = jnp.broadcast_to(rows[:, lane : lane + 1], (16, 128))
        return carry

    lax.fori_loop(0, 8, weights, 0)

    drain(sxr, r_sx)
    for s in range(STEPS):
        edge = [sxr[k, s].astype(F32) for k in range(8)]
        px[s, 0, 8:24] = edge[0]
        px[s, 9, 8:24] = edge[1]
        lo, hi = cut(not_low, edge[2]), cut(not_high, edge[3])
        put_column(px.at[s], 7, lo[8:16])
        put_column(px.at[s], 24, hi[0:8])
        px[s, 0, 7:8] = cut(not_low, edge[4])[15:16]
        px[s, 0, 24:25] = cut(not_high, edge[5])[7:8]
        px[s, 9, 7:8] = cut(not_low, edge[6])[8:9]
        px[s, 9, 24:25] = cut(not_high, edge[7])[0:1]

    def step(it, carry):
        s = STEPS - 1 - it

        @pl.when(it > 0)
        def _():
            halo_send(it)
            accumulate(s + 1)

        halo_fill(it)
        stencil(it, 9)
        spread(it, s)
        forward(s)
        transport(it, s)
        backward(it)
        return carry

    lax.fori_loop(0, STEPS, step, 0)
    halo_send(STEPS)
    accumulate(0)

    for m, acc in enumerate((accd, accu)):
        def pack(j, carry, m=m, acc=acc):
            cs[m, j] = acc[j, :, 1 - core].astype(BF16)
            return carry

        lax.fori_loop(0, LAT, pack, 0)
        send(cs.at[m], cr.at[m], s_c.at[m], r_c.at[m], (mate, lat))

    sums = [jnp.sum(kacc[k], axis=0, keepdims=True) for k in range(9)]
    sums.append(jnp.sum(gacc[...], axis=0, keepdims=True))
    table = jnp.concatenate(sums, axis=0)
    for k in range(GROUPS):
        smc[core, 8 * k : 8 * k + 8, :] = table[0:8, 128 * k : 128 * (k + 1)]
        smc[core, 32 + 2 * k : 34 + 2 * k, :] = table[8:10, 128 * k : 128 * (k + 1)]
    send(smc.at[core], smc.at[core], s_sm.at[0], r_sm.at[0], (mate, lat))

    halo_fill(STEPS)
    stencil(STEPS, 8)
    for i in range(8):
        gs_out[i] = gg[i, 0:16].astype(BF16)

    drain(smc.at[0], r_sm.at[0])
    smy[yy] = smc[0] + smc[1]
    for d in range(1, NY):
        send(smy.at[yy], smy.at[yy], s_sm.at[d], r_sm.at[1], at_y(d))

    for m, acc, dest in ((0, accd, b1d), (1, accu, b1u)):
        drain(cr.at[m], r_c.at[m])

        def join(j, carry, m=m, acc=acc, dest=dest):
            total = acc[j, :, core] + cr[m, j].astype(F32)
            dest[j // NY, lax.rem(j, NY)] = total.astype(BF16).reshape(NX, NZH, 16, 128)
            return carry

        lax.fori_loop(0, LAT, join, 0)
        if m == 0:
            for d in range(1, NX):
                send(b1d.at[:, :, lax.rem(xx + d, NX)], rxd.at[d - 1], s_x.at[0, d - 1], r_x.at[0], at_x(d))
        else:
            for d in range(1, NY):
                send(b1u.at[:, lax.rem(yy + d, NY)], ryu.at[d - 1], s_y.at[1, d - 1], r_y.at[1], at_y(d))

    drain(smy.at[0:3], r_sm.at[1])
    smx[xx] = ((smy[0] + smy[1]) + smy[2]) + smy[3]
    for d in range(1, NX):
        send(smx.at[xx], smx.at[xx], s_sm.at[3 + d], r_sm.at[2], at_x(d))

    drain(rxd, r_x.at[0])
    total = b1d[:, :, xx].astype(F32)
    for d in range(NX - 1):
        total = total + rxd[d].astype(F32)
    b2d[...] = total.astype(BF16)
    for d in range(1, NY):
        send(b2d.at[:, lax.rem(yy + d, NY)], ryd.at[d - 1], s_y.at[0, d - 1], r_y.at[0], at_y(d))

    drain(ryu, r_y.at[1])
    total = b1u[:, yy].astype(F32)
    for d in range(NY - 1):
        total = total + ryu[d].astype(F32)
    b2u[...] = total.astype(BF16)
    for d in range(1, NX):
        send(b2u.at[:, lax.rem(xx + d, NX)], rxu.at[d - 1], s_x.at[1, d - 1], r_x.at[1], at_x(d))

    drain(smx.at[0:3], r_sm.at[2])
    here = zl * NZH + zh
    smz[here] = ((smx[0] + smx[1]) + smx[2]) + smx[3]
    for k, (dzl, dzh) in enumerate(zpairs):
        send(smz.at[here], smz.at[here], s_sm.at[7 + k], r_sm.at[3], at_z(dzl, dzh))

    for m, b1, r2, b2, b3, rz, rsem in (
        (0, None, ryd, b2d, b3d, rzd, r_y.at[0]),
        (1, None, rxu, b2u, b3u, rzu, r_x.at[1]),
    ):
        drain(r2, rsem)
        total = (b2[:, yy] if m == 0 else b2[:, xx]).astype(F32)
        for d in range(3):
            total = total + r2[d].astype(F32)
        b3[...] = total.astype(BF16)
        for k, (dzl, dzh) in enumerate(zpairs):
            send(
                b3.at[lax.rem(zl + dzl, NZL), lax.rem(zh + dzh, NZH)], rz.at[k],
                s_z.at[m, k], r_z.at[m], at_z(dzl, dzh),
            )

    drain(smz.at[0:7], r_sm.at[3])
    total = smz[0]
    for k in range(1, 8):
        total = total + smz[k]
    for k in range(GROUPS):
        kern_out[0:8, 128 * k : 128 * (k + 1)] = total[8 * k : 8 * k + 8]
        kern_out[8:9, 128 * k : 128 * (k + 1)] = total[32 + 2 * k : 33 + 2 * k]
        gain_out[:, 128 * k : 128 * (k + 1)] = total[33 + 2 * k : 34 + 2 * k]

    for m, b3, rz, out in ((0, b3d, rzd, dn_out), (1, b3u, rzu, up_out)):
        drain(rz, r_z.at[m])
        total = b3[zl, zh].astype(F32)
        for k in range(7):
            total = total + rz[k].astype(F32)
        out[...] = total

    for k in range(8):
        drain(sxs, s_sx.at[k])
    drain(bt.at[0:16], s_bt.at[0])
    drain(bt, s_bt.at[1])
    drain(bt.at[0:8], s_bt.at[2])

    def sent(it, carry):
        halo_sent(it)
        for g in range(GROUPS):
            drain(win.at[it, g, 1 : AHEAD + 1], s_l.at[it, g])
            drain(ps.at[it, g], s_p.at[it, g])
            drain(lw.at[it, g], s_t.at[it, g])
        return carry

    lax.fori_loop(0, STEPS, sent, 0)
    halo_sent(STEPS)
    for m in range(2):
        drain(cs.at[m], s_c.at[m])
        for k in range(7):
            drain(b3u.at[0, 0], s_z.at[m, k])
    for d in range(3):
        drain(rxd.at[0], s_x.at[0, d])
        drain(rxu.at[0], s_x.at[1, d])
        drain(ryd.at[0], s_y.at[0, d])
        drain(ryu.at[0], s_y.at[1, d])
    for k in range(14):
        drain(smc.at[0], s_sm.at[k])


def local(cotangent, states, w_up, w_down, norm_gain, kernel_taps, bilinear, lon_move, lat_move):
    table = jnp.transpose(bilinear.reshape(4 * STEPS, 128))
    table = jnp.pad(table, ((0, 0), (0, 128 - 4 * STEPS)))
    vm, sm = pltpu.VMEM, pltpu.SemaphoreType.DMA
    scratch = [
        vm((STEPS, 10, PW, 512), F32),
        vm((11, PW, 512), F32),
        vm((9, GW, 512), F32),
        vm((STEPS, 4, 8, 16, 128), F32),
        vm((9, GW, 128), F32),
        vm((STEPS + 1, 8, 16, 512), BF16),
        vm((STEPS + 1, 2, 16, 512), BF16),
        vm((STEPS + 1, 9, 16, 512), BF16),
        vm((STEPS, 16, 512), BF16),
        vm((8, STEPS, 16, 512), BF16),
        vm((16, 128), F32),
        vm((128, 128), F32),
        vm((8, 128), F32),
        vm((STEPS, GROUPS, AHEAD + 1, 8, 16, 128), BF16),
        vm((GROUPS, AHEAD + 1, 8, 16, 128), BF16),
        vm((STEPS, GROUPS, 8, 16, 128), BF16),
        vm((STEPS, GROUPS, 8, 16, 128), BF16),
        vm((GROUPS, 24, 16, 128), BF16),
        vm((STEPS, GROUPS, 8, 16, 128), BF16),
        vm((STEPS, GROUPS, 2, 8, 16, 128), BF16),
        vm((GROUPS, 8, 48, 128), BF16),
        vm((128, 8 * 48), jnp.int32),
        vm((128, 512), BF16),
        vm((128, 512), BF16),
        vm((8, 128, 128), BF16),
        vm((8, 128, 128), F32),
        vm((128, 512), F32),
        vm((128, 128), F32),
        vm((8, 128, 128), BF16),
        vm((128, 512), F32),
        vm((LAT, 16, 2, 16, 128), F32),
        vm((LAT, 16, 2, 16, 128), F32),
        vm((9, 8, 512), F32),
        vm((8, 512), F32),
        vm((2, LAT, 16, 16, 128), BF16),
        vm((2, LAT, 16, 16, 128), BF16),
        vm((NZL, NY, NX, NZH, 16, 128), BF16),
        vm((3, NZL, NX, NZH, 16, 128), BF16),
        vm((NZL, NX, NZH, 16, 128), BF16),
        vm((3, NZL, NZH, 16, 128), BF16),
        vm((NZL, NZH, 16, 128), BF16),
        vm((7, 16, 128), BF16),
        vm((NZL, NY, NX, NZH, 16, 128), BF16),
        vm((3, NZL, NY, NZH, 16, 128), BF16),
        vm((NZL, NY, NZH, 16, 128), BF16),
        vm((3, NZL, NZH, 16, 128), BF16),
        vm((NZL, NZH, 16, 128), BF16),
        vm((7, 16, 128), BF16),
        vm((2, 40, 128), F32),
        vm((NY, 40, 128), F32),
        vm((NX, 40, 128), F32),
        vm((NZL * NZH, 40, 128), F32),
        sm((8,)), sm, sm((3,)), sm((3,)),
        sm((STEPS + 1, 8)), sm((STEPS + 1,)),
        sm((STEPS, GROUPS)), sm((STEPS, GROUPS)),
        sm((STEPS, GROUPS)), sm((STEPS, GROUPS)),
        sm((STEPS, GROUPS)), sm((STEPS, GROUPS)),
        sm((2,)), sm((2,)),
        sm((2, 3)), sm((2,)), sm((2, 3)), sm((2,)), sm((2, 7)), sm((2,)),
        sm((14,)), sm((4,)),
    ]
    vmem = pl.BlockSpec(memory_space=pltpu.VMEM)
    smem = pl.BlockSpec(memory_space=pltpu.SMEM)
    grad_state, grad_up, grad_down, grad_kernel, grad_gain = pl.pallas_call(
        kernel,
        out_shape=(
            jax.ShapeDtypeStruct((8, 16, 512), BF16),
            jax.ShapeDtypeStruct((16, 128), F32),
            jax.ShapeDtypeStruct((16, 128), F32),
            jax.ShapeDtypeStruct((9, 512), F32),
            jax.ShapeDtypeStruct((1, 512), F32),
        ),
        in_specs=[vmem] * 7 + [smem] * 2,
        out_specs=(vmem,) * 5,
        scratch_shapes=scratch,
        compiler_params=pltpu.CompilerParams(
            collective_id=0, has_side_effects=True, vmem_limit_bytes=56 * 1024 * 1024
        ),
    )(
        cotangent, states, w_up, w_down, norm_gain.reshape(1, 512),
        kernel_taps.reshape(9, 512), table, lon_move, lat_move,
    )
    return (
        grad_state, grad_up, grad_down, grad_kernel.reshape(3, 3, 512), grad_gain.reshape(512)
    )


def solution(mesh):
    placed = (
        P("lon", "lat", None),
        P(None, "lon", "lat", None),
        P(),
        P(),
        P(),
        P(),
        P(None, None, "lon", "lat"),
        P(),
        P(),
    )
    return jax.shard_map(
        local,
        mesh=mesh,
        in_specs=placed,
        out_specs=(P("lon", "lat", None), P("lon", "lat"), P("lon", "lat"), P(), P()),
        check_vma=False,
    )
```

```python
import jax
import jax.numpy as jnp
from jax import lax
from jax.experimental import pallas as pl
from jax.experimental.pallas import tpu as pltpu
from jax.sharding import PartitionSpec as P

GROUPS = 4
STEPS = 3
EPSILON = 1e-06
MESH = pl.DeviceIdType.MESH
F32 = jnp.float32
BF16 = jnp.bfloat16

NX, NZH, NZL, NY = 4, 4, 2, 4
LON, LAT = NX * NZH * 2, NZL * NY
AHEAD = 4
PW = 32
GW = 24


def kernel(
    cot, st, wu_hbm, wd_hbm, gain, kern, bil, lm, lt,
    gs_out, up_out, dn_out, kern_out, gain_out,
    wu, wd, px, pf, gg, wb, square, bt, pt, fld, stg, hb, sxs, sxr, br,
    win, near_by, ps, pr, lon2, lb, lw, lwin, diff,
    mv, nn, hid, ds, nrm, inv, gp, gn, accu, accd, kacc, gacc,
    cs, cr, b1u, ryu, b2u, rxu, b3u, rzu, b1d, rxd, b2d, ryd, b3d, rzd,
    smc, smy, smx, smz,
    s_w, s_sx, r_sx, s_bt, r_bt, s_h, r_h, s_l, r_l, s_p, r_p, s_t, r_t,
    s_c, r_c, s_y, r_y, s_x, r_x, s_z, r_z, s_sm, r_sm,
):
    lon = lax.axis_index("lon")
    lat = lax.axis_index("lat")
    core = lax.rem(lon, 2)
    chip = lon // 2
    xx, zh = chip // NZH, lax.rem(chip, NZH)
    zl, yy = lat // NY, lax.rem(lat, NY)
    mate = lon + 1 - 2 * core

    def at(dlon, dlat):
        return (lax.rem(lon + dlon + LON, LON), lax.rem(lat + dlat + LAT, LAT))

    def at_y(d):
        return (lon, zl * NY + lax.rem(yy + d, NY))

    def at_x(d):
        return (lax.rem(xx + d, NX) * (2 * NZH) + zh * 2 + core, lat)

    def at_z(dzl, dzh):
        return (
            (xx * NZH + lax.rem(zh + dzh, NZH)) * 2 + core,
            lax.rem(zl + dzl, NZL) * NY + yy,
        )

    def send(src, dst, ssem, rsem, target):
        pltpu.make_async_remote_copy(
            src_ref=src, dst_ref=dst, send_sem=ssem, recv_sem=rsem,
            device_id=target, device_id_type=MESH,
        ).start()

    def drain(ref, sem):
        pltpu.make_async_copy(ref, ref, sem).wait()

    near = [(a, b) for a in (-1, 0, 1) for b in (-1, 0, 1) if (a, b) != (0, 0)]
    zpairs = [(a, b) for a in range(NZL) for b in range(NZH) if (a, b) != (0, 0)]
    partners = [at(a, b) for a, b in near]
    partners += [at(2 * d * sign, 0) for d in range(1, AHEAD + 1) for sign in (-1, 1)]
    partners += [at(0, 2), at(0, -2)]
    partners += [at_y(d) for d in range(1, NY)] + [at_x(d) for d in range(1, NX)]
    partners += [at_z(a, b) for a, b in zpairs]
    barrier = pltpu.get_barrier_semaphore()
    for target in partners:
        pl.semaphore_signal(barrier, inc=1, device_id=target, device_id_type=MESH)

    def column(ref, j):
        return [ref[i, j : j + 1] for i in range(1, 9)]

    def put_column(ref, j, rows):
        for i in range(8):
            ref[i + 1, j : j + 1] = rows[i : i + 1]

    fetch = [
        pltpu.make_async_copy(wu_hbm, wu, s_w.at[0]), pltpu.make_async_copy(wd_hbm, wd, s_w.at[1])
    ]
    for copy in fetch:
        copy.start()

    not_low = lat > 0
    not_high = lat < LAT - 1
    for i in range(8):
        block = cot[i]
        fld[0, i] = block
        pf[i + 1, 8:24] = block.astype(F32)
        for s in range(STEPS):
            px[s, i + 1, 8:24] = st[s, i].astype(F32)
    for s in range(STEPS):
        sxs[s] = jnp.concatenate(
            column(px.at[s], 8) + column(px.at[s], 23), axis=0
        ).astype(BF16)
    square[...] = jnp.zeros_like(square)
    square[0 : 32 * STEPS, 0:16] = bil[...].reshape(32 * STEPS, 16)
    bt[...] = jnp.transpose(square[...])[0:16]
    place = lax.broadcasted_iota(jnp.int32, diff.shape, 0)
    diff[...] = (
        lax.broadcasted_iota(jnp.int32, diff.shape, 1)
        - lax.div(place, 16) * 48 - lax.rem(place, 16)
    )
    pl.semaphore_wait(barrier, len(partners))

    def halo_send(it):
        first, second, last = column(pf, 8), column(pf, 9), column(pf, 23)
        stg[it, 0] = jnp.concatenate(first + second, axis=0).astype(BF16)
        stg[it, 1] = jnp.concatenate(last + last, axis=0).astype(BF16)
        low, high = stg.at[it, 0], stg.at[it, 1]

        def go(src, block, target, k):
            send(src, hb.at[it, block], s_h.at[it, k], r_h.at[it], target)

        send(fld.at[it, 0:2], hb.at[it, 1:3], s_h.at[it, 1], r_h.at[it], at(-1, 0))
        go(fld.at[it, 7], 0, at(1, 0), 0)
        go(high, 3, at(0, 1), 2)
        go(low, 4, at(0, -1), 3)
        go(high, 5, at(1, 1), 4)
        go(low, 6, at(1, -1), 5)
        go(high, 7, at(-1, 1), 6)
        go(low, 8, at(-1, -1), 7)

    def halo_sent(it):
        drain(fld.at[it, 7], s_h.at[it, 0])
        drain(fld.at[it, 0:2], s_h.at[it, 1])
        for k in range(2, 8):
            drain(stg.at[it, 0], s_h.at[it, k])

    def cut(keep, value):
        return jnp.where(keep, value, jnp.zeros_like(value))

    def halo_fill(it):
        drain(hb.at[it], r_h.at[it])
        block = [hb[it, k].astype(F32) for k in range(9)]
        pf[0, 8:24] = block[0]
        pf[9, 8:24] = block[1]
        pf[10, 8:24] = block[2]
        lo, hi = cut(not_low, block[3]), cut(not_high, block[4])
        put_column(pf, 7, lo[8:16])
        put_column(pf, 24, hi[0:8])
        put_column(pf, 25, hi[8:16])
        lo, hi = cut(not_low, block[5]), cut(not_high, block[6])
        pf[0, 7:8] = lo[15:16]
        pf[0, 24:25] = hi[7:8]
        pf[0, 25:26] = hi[15:16]
        lo, hi = cut(not_low, block[7]), cut(not_high, block[8])
        for r in (9, 10):
            pf[r, 7:8] = lo[8 + r - 9 : 8 + r - 8]
            pf[r, 24:25] = hi[r - 9 : r - 8]
            pf[r, 25:26] = hi[8 + r - 9 : 8 + r - 8]

    def stencil(it, rows):
        on = jnp.where(it > 0, 1.0, 0.0).astype(F32)

        def row(i, carry):
            for k in range(GROUPS):
                lanes = pl.ds(128 * k, 128)
                total = pf[i + 1, 8 : 6 + GW, lanes]
                centre = total
                running = jnp.zeros_like(total)
                for a in range(3):
                    for b in range(3):
                        tap = kern[a, b : b + 1, lanes] * on
                        running = running + tap * (
                            pf[i + 2 - a, 9 - b : 9 - b + GW - 2, lanes]
                        )
                gg[i, 0 : GW - 2, lanes] = (centre + running).astype(BF16).astype(F32)
            return carry

        lax.fori_loop(0, rows, row, 0)

    def accumulate(s):
        def block(j, carry):
            pair = jnp.concatenate([gp[2 * j], gp[2 * j + 1]], axis=1)
            part = lax.dot_general(
                nn[...], pair, (((0,), (0,)), ((), ())), preferred_element_type=F32
            )
            accu[2 * j] += part[:, :128].reshape(16, 2, 16, 128)
            accu[2 * j + 1] += part[:, 128:].reshape(16, 2, 16, 128)
            pair = jnp.concatenate([hid[2 * j], hid[2 * j + 1]], axis=1)
            part = lax.dot_general(
                mv[...], pair, (((0,), (0,)), ((), ())), preferred_element_type=F32
            )
            accd[2 * j] += part[:, :128].reshape(16, 2, 16, 128)
            accd[2 * j + 1] += part[:, 128:].reshape(16, 2, 16, 128)
            return carry

        lax.fori_loop(0, 4, block, 0)

        def row(i, carry):
            f = pf[i + 1, 8:24]
            for a in range(3):
                for b in range(3):
                    prod = px[s, i + a, 7 + b : 23 + b] * f
                    kacc[3 * a + b] += prod[:8] + prod[8:]
            rows = pl.ds(pl.multiple_of(i * 16, 16), 16)
            prod = gn[rows, :] * nrm[rows, :]
            gacc[...] += prod[:8] + prod[8:]
            return carry

        lax.fori_loop(0, 8, row, 0)

    def spread(it, s):
        for k in range(GROUPS):
            lanes = pl.ds(128 * k, 128)

            def row(i, carry):
                own = wb[s, 0, i] * gg[i, 0:16, lanes]
                own = own + wb[s, 1, i] * gg[i + 1, 0:16, lanes]
                own = own + wb[s, 2, i] * gg[i, 1:17, lanes]
                own = own + wb[s, 3, i] * gg[i + 1, 1:17, lanes]
                win[it, k, 0, i] = own.astype(BF16)
                return carry

            lax.fori_loop(0, 8, row, 0)
            for d in range(1, AHEAD + 1):
                send(
                    win.at[it, k, 0], win.at[it, k, d], s_l.at[it, k], r_l.at[it, k],
                    at(-2 * d, 0),
                )

    def forward(s):
        def row(i, carry):
            u = px[s, i + 1, 8:24]
            running = jnp.zeros_like(u)
            for a in range(3):
                for b in range(3):
                    running = running + kern[a, b : b + 1, :] * (
                        px[s, i + a, 7 + b : 23 + b]
                    )
            u = u + running
            root = lax.rsqrt(jnp.mean(u * u, axis=-1, keepdims=True) + EPSILON)
            rows = pl.ds(pl.multiple_of(i * 16, 16), 16)
            normed = u * root
            nrm[rows, :] = normed
            inv[rows, :] = jnp.broadcast_to(root, (16, 128))
            nn[rows, :] = (normed * gain[...]).astype(BF16)
            return carry

        lax.fori_loop(0, 8, row, 0)

        def block(j, carry):
            cols = pl.ds(pl.multiple_of(j * 256, 256), 256)
            pre = jnp.dot(nn[...], wu[:, cols], preferred_element_type=F32)
            sig = jax.nn.sigmoid(pre)
            hidden = (pre * sig).astype(BF16)
            slope = sig * (1.0 + pre * (1.0 - sig))
            for h in range(2):
                hid[2 * j + h] = hidden[:, 128 * h : 128 * (h + 1)]
                ds[2 * j + h] = slope[:, 128 * h : 128 * (h + 1)]
            return carry

        lax.fori_loop(0, 4, block, 0)

    def transport(it, s):
        for k in range(GROUPS + 2):
            if k < GROUPS:
                g = k
                drain(win.at[it, g, 1 : AHEAD + 1], r_l.at[it, g])
                for d in range(AHEAD + 1):
                    near_by[g, d] = win[it, g, d]
                far = lax.div(lm[s, g], 8)
                ps[it, g] = near_by[g, lax.div(far, 2) + 1 - core]
                send(ps.at[it, g], pr.at[it, g], s_p.at[it, g], r_p.at[it, g], (mate, lat))
            if 1 <= k <= GROUPS:
                g = k - 1
                drain(pr.at[it, g], r_p.at[it, g])
                move = lm[s, g]
                far = lax.div(move, 8)
                odd = pr[it, g]
                lon2[g, 0:8] = odd
                lon2[g, 8:16] = near_by[g, lax.div(far + 1, 2)]
                lon2[g, 16:24] = odd
                begin = 8 - 8 * lax.rem(far, 2) + lax.rem(move, 8)
                for i in range(8):
                    own = lon2[g, begin + i]
                    lb[it, g, i] = own
                    lwin[g, i, 0:16] = own
                for d in (1, 2):
                    send(
                        lb.at[it, g], lw.at[it, g, d - 1], s_t.at[it, g], r_t.at[it, g],
                        at(0, -d),
                    )
            if k >= 2:
                g = k - 2
                drain(lw.at[it, g], r_t.at[it, g])
                lwin[g, :, 16:32] = cut(lat < LAT - 1, lw[it, g, 0])
                lwin[g, :, 32:48] = cut(lat < LAT - 2, lw[it, g, 1])
                pick = jnp.where(diff[...] == lt[s, g], 1.0, 0.0).astype(BF16)
                mv[:, 128 * g : 128 * (g + 1)] = jnp.dot(
                    pick, lwin[g].reshape(8 * 48, 128), preferred_element_type=F32
                ).astype(BF16)

    def backward(it):
        total = None
        for j in range(4):
            cols = slice(256 * j, 256 * (j + 1))
            up = jnp.dot(mv[...], wd[:, cols], preferred_element_type=F32)
            slope = jnp.concatenate([ds[2 * j], ds[2 * j + 1]], axis=1)
            pre = (up * slope).astype(BF16)
            gp[2 * j] = pre[:, :128]
            gp[2 * j + 1] = pre[:, 128:]
            part = lax.dot_general(
                pre, wu[:, cols], (((1,), (1,)), ((), ())), preferred_element_type=F32
            )
            total = part if total is None else total + part
        gn[...] = total

        def row(i, carry):
            rows = pl.ds(pl.multiple_of(i * 16, 16), 16)
            normed = nrm[rows, :]
            scaled = gn[rows, :] * gain[...]
            mean = jnp.mean(scaled * normed, axis=-1, keepdims=True)
            root = jnp.concatenate([inv[rows, :]] * GROUPS, axis=1)
            field = (mv[rows, :].astype(F32) + root * (scaled - normed * mean)).astype(BF16)
            fld[it + 1, i] = field
            pf[i + 1, 8:24] = field.astype(F32)
            return carry

        lax.fori_loop(0, 8, row, 0)

    halo_send(0)
    for k, (a, b) in enumerate(((-1, 0), (0, -1), (-1, -1))):
        send(bt, br.at[k], s_bt.at[k], r_bt, at(a, b))
    state_edges = [
        (st.at[:, 7], at(1, 0)), (st.at[:, 0], at(-1, 0)), (sxs, at(0, 1)), (sxs, at(0, -1)),
        (sxs, at(1, 1)), (sxs, at(1, -1)), (sxs, at(-1, 1)), (sxs, at(-1, -1)),
    ]
    for k, (src, target) in enumerate(state_edges):
        send(src, sxr.at[k], s_sx.at[k], r_sx, target)

    accu[...] = jnp.zeros_like(accu)
    accd[...] = jnp.zeros_like(accd)
    kacc[...] = jnp.zeros_like(kacc)
    gacc[...] = jnp.zeros_like(gacc)

    drain(br, r_bt)
    pt[0, 0:16] = bt[...]
    pt[0, 16:17] = cut(not_high, br[1, 0:1])
    pt[1, 0:16] = br[0]
    pt[1, 16:17] = cut(not_high, br[2, 0:1])
    for i in range(8):
        for q, (di, dj) in enumerate(((0, 0), (1, 0), (0, 1), (1, 1))):
            rows = pt[(i + di) // 8, dj : dj + 16]
            for s in range(STEPS):
                lane = (4 * s + q) * 8 + (i + di) % 8
                wb[s, q, i] = jnp.broadcast_to(rows[:, lane : lane + 1], (16, 128))

    drain(sxr, r_sx)
    for s in range(STEPS):
        edge = [sxr[k, s].astype(F32) for k in range(8)]
        px[s, 0, 8:24] = edge[0]
        px[s, 9, 8:24] = edge[1]
        lo, hi = cut(not_low, edge[2]), cut(not_high, edge[3])
        put_column(px.at[s], 7, lo[8:16])
        put_column(px.at[s], 24, hi[0:8])
        px[s, 0, 7:8] = cut(not_low, edge[4])[15:16]
        px[s, 0, 24:25] = cut(not_high, edge[5])[7:8]
        px[s, 9, 7:8] = cut(not_low, edge[6])[8:9]
        px[s, 9, 24:25] = cut(not_high, edge[7])[0:1]

    for copy in fetch:
        copy.wait()

    def step(it, carry):
        s = STEPS - 1 - it

        @pl.when(it > 0)
        def _():
            halo_send(it)
            accumulate(s + 1)

        halo_fill(it)
        stencil(it, 9)
        spread(it, s)
        forward(s)
        transport(it, s)
        backward(it)
        return carry

    lax.fori_loop(0, STEPS, step, 0)
    halo_send(STEPS)
    accumulate(0)

    for m, acc in enumerate((accd, accu)):
        def pack(j, carry, m=m, acc=acc):
            cs[m, j] = acc[j, :, 1 - core].astype(BF16)
            return carry

        lax.fori_loop(0, LAT, pack, 0)
        send(cs.at[m], cr.at[m], s_c.at[m], r_c.at[m], (mate, lat))

    sums = [jnp.sum(kacc[k], axis=0, keepdims=True) for k in range(9)]
    sums.append(jnp.sum(gacc[...], axis=0, keepdims=True))
    table = jnp.concatenate(sums, axis=0)
    for k in range(GROUPS):
        smc[core, 8 * k : 8 * k + 8, :] = table[0:8, 128 * k : 128 * (k + 1)]
        smc[core, 32 + 2 * k : 34 + 2 * k, :] = table[8:10, 128 * k : 128 * (k + 1)]
    send(smc.at[core], smc.at[core], s_sm.at[0], r_sm.at[0], (mate, lat))

    halo_fill(STEPS)
    stencil(STEPS, 8)
    for i in range(8):
        gs_out[i] = gg[i, 0:16].astype(BF16)

    drain(smc.at[0], r_sm.at[0])
    smy[yy] = smc[0] + smc[1]
    for d in range(1, NY):
        send(smy.at[yy], smy.at[yy], s_sm.at[d], r_sm.at[1], at_y(d))

    for m, acc, dest in ((0, accd, b1d), (1, accu, b1u)):
        drain(cr.at[m], r_c.at[m])

        def join(j, carry, m=m, acc=acc, dest=dest):
            total = acc[j, :, core] + cr[m, j].astype(F32)
            dest[j // NY, lax.rem(j, NY)] = total.astype(BF16).reshape(NX, NZH, 16, 128)
            return carry

        lax.fori_loop(0, LAT, join, 0)
        if m == 0:
            for d in range(1, NX):
                send(b1d.at[:, :, lax.rem(xx + d, NX)], rxd.at[d - 1], s_x.at[0, d - 1], r_x.at[0], at_x(d))
        else:
            for d in range(1, NY):
                send(b1u.at[:, lax.rem(yy + d, NY)], ryu.at[d - 1], s_y.at[1, d - 1], r_y.at[1], at_y(d))

    drain(smy.at[0:3], r_sm.at[1])
    smx[xx] = ((smy[0] + smy[1]) + smy[2]) + smy[3]
    for d in range(1, NX):
        send(smx.at[xx], smx.at[xx], s_sm.at[3 + d], r_sm.at[2], at_x(d))

    drain(rxd, r_x.at[0])
    total = b1d[:, :, xx].astype(F32)
    for d in range(NX - 1):
        total = total + rxd[d].astype(F32)
    b2d[...] = total.astype(BF16)
    for d in range(1, NY):
        send(b2d.at[:, lax.rem(yy + d, NY)], ryd.at[d - 1], s_y.at[0, d - 1], r_y.at[0], at_y(d))

    drain(ryu, r_y.at[1])
    total = b1u[:, yy].astype(F32)
    for d in range(NY - 1):
        total = total + ryu[d].astype(F32)
    b2u[...] = total.astype(BF16)
    for d in range(1, NX):
        send(b2u.at[:, lax.rem(xx + d, NX)], rxu.at[d - 1], s_x.at[1, d - 1], r_x.at[1], at_x(d))

    drain(smx.at[0:3], r_sm.at[2])
    here = zl * NZH + zh
    smz[here] = ((smx[0] + smx[1]) + smx[2]) + smx[3]
    for k, (dzl, dzh) in enumerate(zpairs):
        send(smz.at[here], smz.at[here], s_sm.at[7 + k], r_sm.at[3], at_z(dzl, dzh))

    for m, b1, r2, b2, b3, rz, rsem in (
        (0, None, ryd, b2d, b3d, rzd, r_y.at[0]),
        (1, None, rxu, b2u, b3u, rzu, r_x.at[1]),
    ):
        drain(r2, rsem)
        total = (b2[:, yy] if m == 0 else b2[:, xx]).astype(F32)
        for d in range(3):
            total = total + r2[d].astype(F32)
        b3[...] = total.astype(BF16)
        for k, (dzl, dzh) in enumerate(zpairs):
            send(
                b3.at[lax.rem(zl + dzl, NZL), lax.rem(zh + dzh, NZH)], rz.at[k],
                s_z.at[m, k], r_z.at[m], at_z(dzl, dzh),
            )

    drain(smz.at[0:7], r_sm.at[3])
    total = smz[0]
    for k in range(1, 8):
        total = total + smz[k]
    for k in range(GROUPS):
        for tap in range(9):
            at_row = 8 * k + tap if tap < 8 else 32 + 2 * k
            kern_out[tap // 3, tap % 3 : tap % 3 + 1, 128 * k : 128 * (k + 1)] = (
                total[at_row : at_row + 1]
            )
        gain_out[:, 128 * k : 128 * (k + 1)] = total[33 + 2 * k : 34 + 2 * k]

    for m, b3, rz, out in ((0, b3d, rzd, dn_out), (1, b3u, rzu, up_out)):
        drain(rz, r_z.at[m])
        total = b3[zl, zh].astype(F32)
        for k in range(7):
            total = total + rz[k].astype(F32)
        out[...] = total

    for k in range(8):
        drain(sxs, s_sx.at[k])
    for k in range(3):
        drain(bt, s_bt.at[k])

    def sent(it, carry):
        halo_sent(it)
        for g in range(GROUPS):
            drain(win.at[it, g, 1 : AHEAD + 1], s_l.at[it, g])
            drain(ps.at[it, g], s_p.at[it, g])
            drain(lw.at[it, g], s_t.at[it, g])
        return carry

    lax.fori_loop(0, STEPS, sent, 0)
    halo_sent(STEPS)
    for m in range(2):
        drain(cs.at[m], s_c.at[m])
        for k in range(7):
            drain(b3u.at[0, 0], s_z.at[m, k])
    for d in range(3):
        drain(rxd.at[0], s_x.at[0, d])
        drain(rxu.at[0], s_x.at[1, d])
        drain(ryd.at[0], s_y.at[0, d])
        drain(ryu.at[0], s_y.at[1, d])
    for k in range(14):
        drain(smc.at[0], s_sm.at[k])


def hand_over(*refs):
    for source, result in zip(refs[:5], refs[5:]):
        result[...] = source[...]


def local(cotangent, states, w_up, w_down, norm_gain, kernel_taps, bilinear, lon_move, lat_move):
    vm, sm = pltpu.VMEM, pltpu.SemaphoreType.DMA
    scratch = [
        vm((512, 1024), BF16),
        vm((512, 1024), BF16),
        vm((STEPS, 10, PW, 512), F32),
        vm((11, PW, 512), F32),
        vm((9, GW, 512), F32),
        vm((STEPS, 4, 8, 16, 128), F32),
        vm((128, 128), F32),
        vm((16, 128), F32),
        vm((2, GW, 128), F32),
        vm((STEPS + 1, 8, 16, 512), BF16),
        vm((STEPS + 1, 2, 16, 512), BF16),
        vm((STEPS + 1, 9, 16, 512), BF16),
        vm((STEPS, 16, 512), BF16),
        vm((8, STEPS, 16, 512), BF16),
        vm((3, 16, 128), F32),
        vm((STEPS, GROUPS, AHEAD + 1, 8, 16, 128), BF16),
        vm((GROUPS, AHEAD + 1, 8, 16, 128), BF16),
        vm((STEPS, GROUPS, 8, 16, 128), BF16),
        vm((STEPS, GROUPS, 8, 16, 128), BF16),
        vm((GROUPS, 24, 16, 128), BF16),
        vm((STEPS, GROUPS, 8, 16, 128), BF16),
        vm((STEPS, GROUPS, 2, 8, 16, 128), BF16),
        vm((GROUPS, 8, 48, 128), BF16),
        vm((128, 8 * 48), jnp.int32),
        vm((128, 512), BF16),
        vm((128, 512), BF16),
        vm((8, 128, 128), BF16),
        vm((8, 128, 128), F32),
        vm((128, 512), F32),
        vm((128, 128), F32),
        vm((8, 128, 128), BF16),
        vm((128, 512), F32),
        vm((LAT, 16, 2, 16, 128), F32),
        vm((LAT, 16, 2, 16, 128), F32),
        vm((9, 8, 512), F32),
        vm((8, 512), F32),
        vm((2, LAT, 16, 16, 128), BF16),
        vm((2, LAT, 16, 16, 128), BF16),
        vm((NZL, NY, NX, NZH, 16, 128), BF16),
        vm((3, NZL, NX, NZH, 16, 128), BF16),
        vm((NZL, NX, NZH, 16, 128), BF16),
        vm((3, NZL, NZH, 16, 128), BF16),
        vm((NZL, NZH, 16, 128), BF16),
        vm((7, 16, 128), BF16),
        vm((NZL, NY, NX, NZH, 16, 128), BF16),
        vm((3, NZL, NY, NZH, 16, 128), BF16),
        vm((NZL, NY, NZH, 16, 128), BF16),
        vm((3, NZL, NZH, 16, 128), BF16),
        vm((NZL, NZH, 16, 128), BF16),
        vm((7, 16, 128), BF16),
        vm((2, 40, 128), F32),
        vm((NY, 40, 128), F32),
        vm((NX, 40, 128), F32),
        vm((NZL * NZH, 40, 128), F32),
        sm((2,)), sm((8,)), sm, sm((3,)), sm,
        sm((STEPS + 1, 8)), sm((STEPS + 1,)),
        sm((STEPS, GROUPS)), sm((STEPS, GROUPS)),
        sm((STEPS, GROUPS)), sm((STEPS, GROUPS)),
        sm((STEPS, GROUPS)), sm((STEPS, GROUPS)),
        sm((2,)), sm((2,)),
        sm((2, 3)), sm((2,)), sm((2, 3)), sm((2,)), sm((2, 7)), sm((2,)),
        sm((14,)), sm((4,)),
    ]
    vmem = pl.BlockSpec(memory_space=pltpu.VMEM)
    smem = pl.BlockSpec(memory_space=pltpu.SMEM)
    anywhere = pl.BlockSpec(memory_space=pl.ANY)
    swept = pl.pallas_call(
        kernel,
        out_shape=(
            jax.ShapeDtypeStruct((8, 16, 512), BF16),
            jax.ShapeDtypeStruct((16, 128), F32),
            jax.ShapeDtypeStruct((16, 128), F32),
            jax.ShapeDtypeStruct((3, 3, 512), F32),
            jax.ShapeDtypeStruct((1, 512), F32),
        ),
        in_specs=[vmem] * 2 + [anywhere] * 2 + [vmem] * 3 + [smem] * 2,
        out_specs=(vmem,) * 5,
        scratch_shapes=scratch,
        compiler_params=pltpu.CompilerParams(
            collective_id=0, has_side_effects=True, vmem_limit_bytes=56 * 1024 * 1024
        ),
    )(
        cotangent, states, w_up, w_down, norm_gain.reshape(1, 512),
        kernel_taps, bilinear, lon_move, lat_move,
    )
    grad_state, grad_up, grad_down, grad_kernel, grad_gain = pl.pallas_call(
        hand_over,
        out_shape=tuple(jax.ShapeDtypeStruct(a.shape, a.dtype) for a in swept),
        in_specs=[vmem] * 5,
        out_specs=(vmem,) * 5,
    )(*swept)
    return (grad_state, grad_up, grad_down, grad_kernel, grad_gain.reshape(512))


def solution(mesh):
    placed = (
        P("lon", "lat", None),
        P(None, "lon", "lat", None),
        P(),
        P(),
        P(),
        P(),
        P(None, None, "lon", "lat"),
        P(),
        P(),
    )
    return jax.shard_map(
        local,
        mesh=mesh,
        in_specs=placed,
        out_specs=(P("lon", "lat", None), P("lon", "lat"), P("lon", "lat"), P(), P()),
        check_vma=False,
    )
```

```python
import jax
import jax.numpy as jnp
from jax import lax
from jax.experimental import pallas as pl
from jax.experimental.pallas import tpu as pltpu
from jax.sharding import PartitionSpec as P

GROUPS = 4
STEPS = 3
EPSILON = 1e-06
MESH = pl.DeviceIdType.MESH
F32 = jnp.float32
BF16 = jnp.bfloat16

NX, NZH, NZL, NY = 4, 4, 2, 4
LON, LAT = NX * NZH * 2, NZL * NY
AHEAD = 4
PW = 32
GW = 24


def kernel(
    cot, st, wu_hbm, wd_hbm, gain, kern, bil, lm, lt,
    gs_out, up_out, dn_out, kern_out, gain_out,
    wu, wd, px, pf, gg, wb, square, bt, pt, fld, stg, hb, sxs, sxr, br,
    win, near_by, ps, pr, lon2, lb, lw, lwin, diff,
    mv, mr, nn, nr, hid, hr, gp, gr, ds, nrm, inv, gn, accu, accd, kacc, gacc,
    b1u, ryu, b2u, rxu, b3u, rzu, b1d, rxd, b2d, ryd, b3d, rzd,
    smc, smy, smx, smz,
    s_w, s_sx, r_sx, s_bt, r_bt, s_h, r_h, s_l, r_l, s_p, r_p, s_t, r_t,
    s_e, r_e, s_y, r_y, s_x, r_x, s_z, r_z, s_sm, r_sm,
):
    lon = lax.axis_index("lon")
    lat = lax.axis_index("lat")
    core = lax.rem(lon, 2)
    chip = lon // 2
    xx, zh = chip // NZH, lax.rem(chip, NZH)
    zl, yy = lat // NY, lax.rem(lat, NY)
    mate = lon + 1 - 2 * core

    def at(dlon, dlat):
        return (lax.rem(lon + dlon + LON, LON), lax.rem(lat + dlat + LAT, LAT))

    def at_y(d):
        return (lon, zl * NY + lax.rem(yy + d, NY))

    def at_x(d):
        return (lax.rem(xx + d, NX) * (2 * NZH) + zh * 2 + core, lat)

    def at_z(dzl, dzh):
        return (
            (xx * NZH + lax.rem(zh + dzh, NZH)) * 2 + core,
            lax.rem(zl + dzl, NZL) * NY + yy,
        )

    def at_pillar(dzl, dzh, dcore):
        return (
            (xx * NZH + lax.rem(zh + dzh, NZH)) * 2 + lax.rem(core + dcore, 2),
            lax.rem(zl + dzl, NZL) * NY + yy,
        )

    def send(src, dst, ssem, rsem, target):
        pltpu.make_async_remote_copy(
            src_ref=src, dst_ref=dst, send_sem=ssem, recv_sem=rsem,
            device_id=target, device_id_type=MESH,
        ).start()

    def drain(ref, sem):
        pltpu.make_async_copy(ref, ref, sem).wait()

    near = [(a, b) for a in (-1, 0, 1) for b in (-1, 0, 1) if (a, b) != (0, 0)]
    zpairs = [(a, b) for a in range(NZL) for b in range(NZH) if (a, b) != (0, 0)]
    pillar = [(a, b, c) for a in range(NZL) for b in range(NZH) for c in range(2) if a + b + c]
    partners = [at(a, b) for a, b in near]
    partners += [at(2 * d * sign, 0) for d in range(1, AHEAD + 1) for sign in (-1, 1)]
    partners += [at(0, 2), at(0, -2)]
    partners += [at_y(d) for d in range(1, NY)] + [at_x(d) for d in range(1, NX)]
    partners += [at_pillar(a, b, c) for a, b, c in pillar]
    barrier = pltpu.get_barrier_semaphore()
    for target in partners:
        pl.semaphore_signal(barrier, inc=1, device_id=target, device_id_type=MESH)

    def column(ref, j):
        return [ref[i, j : j + 1] for i in range(1, 9)]

    def put_column(ref, j, rows):
        for i in range(8):
            ref[i + 1, j : j + 1] = rows[i : i + 1]

    fetch = [
        pltpu.make_async_copy(wu_hbm, wu, s_w.at[0]), pltpu.make_async_copy(wd_hbm, wd, s_w.at[1])
    ]
    for copy in fetch:
        copy.start()

    not_low = lat > 0
    not_high = lat < LAT - 1
    for i in range(8):
        block = cot[i]
        fld[0, i] = block
        pf[i + 1, 8:24] = block.astype(F32)
        for s in range(STEPS):
            px[s, i + 1, 8:24] = st[s, i].astype(F32)
    for s in range(STEPS):
        sxs[s] = jnp.concatenate(
            column(px.at[s], 8) + column(px.at[s], 23), axis=0
        ).astype(BF16)
    square[...] = jnp.zeros_like(square)
    square[0 : 32 * STEPS, 0:16] = bil[...].reshape(32 * STEPS, 16)
    bt[...] = jnp.transpose(square[...])[0:16]
    place = lax.broadcasted_iota(jnp.int32, diff.shape, 0)
    diff[...] = (
        lax.broadcasted_iota(jnp.int32, diff.shape, 1)
        - lax.div(place, 16) * 48 - lax.rem(place, 16)
    )
    pl.semaphore_wait(barrier, len(partners))

    def halo_send(it):
        first, second, last = column(pf, 8), column(pf, 9), column(pf, 23)
        stg[it, 0] = jnp.concatenate(first + second, axis=0).astype(BF16)
        stg[it, 1] = jnp.concatenate(last + last, axis=0).astype(BF16)
        low, high = stg.at[it, 0], stg.at[it, 1]

        def go(src, block, target, k):
            send(src, hb.at[it, block], s_h.at[it, k], r_h.at[it], target)

        send(fld.at[it, 0:2], hb.at[it, 1:3], s_h.at[it, 1], r_h.at[it], at(-1, 0))
        go(fld.at[it, 7], 0, at(1, 0), 0)
        go(high, 3, at(0, 1), 2)
        go(low, 4, at(0, -1), 3)
        go(high, 5, at(1, 1), 4)
        go(low, 6, at(1, -1), 5)
        go(high, 7, at(-1, 1), 6)
        go(low, 8, at(-1, -1), 7)

    def halo_sent(it):
        drain(fld.at[it, 7], s_h.at[it, 0])
        drain(fld.at[it, 0:2], s_h.at[it, 1])
        for k in range(2, 8):
            drain(stg.at[it, 0], s_h.at[it, k])

    def cut(keep, value):
        return jnp.where(keep, value, jnp.zeros_like(value))

    def halo_fill(it):
        drain(hb.at[it], r_h.at[it])
        block = [hb[it, k].astype(F32) for k in range(9)]
        pf[0, 8:24] = block[0]
        pf[9, 8:24] = block[1]
        pf[10, 8:24] = block[2]
        lo, hi = cut(not_low, block[3]), cut(not_high, block[4])
        put_column(pf, 7, lo[8:16])
        put_column(pf, 24, hi[0:8])
        put_column(pf, 25, hi[8:16])
        lo, hi = cut(not_low, block[5]), cut(not_high, block[6])
        pf[0, 7:8] = lo[15:16]
        pf[0, 24:25] = hi[7:8]
        pf[0, 25:26] = hi[15:16]
        lo, hi = cut(not_low, block[7]), cut(not_high, block[8])
        for r in (9, 10):
            pf[r, 7:8] = lo[8 + r - 9 : 8 + r - 8]
            pf[r, 24:25] = hi[r - 9 : r - 8]
            pf[r, 25:26] = hi[8 + r - 9 : 8 + r - 8]

    def stencil(it, rows, k):
        on = jnp.where(it > 0, 1.0, 0.0).astype(F32)
        lanes = pl.ds(128 * k, 128)

        def row(i, carry):
            centre = pf[i + 1, 8 : 6 + GW, lanes]
            running = jnp.zeros_like(centre)
            for a in range(3):
                for b in range(3):
                    tap = kern[a, b : b + 1, lanes] * on
                    running = running + tap * (
                        pf[i + 2 - a, 9 - b : 9 - b + GW - 2, lanes]
                    )
            gg[i, 0 : GW - 2, lanes] = (centre + running).astype(BF16).astype(F32)
            return carry

        lax.fori_loop(0, rows, row, 0)

    def exchange(src, dst, it, k):
        send(src, dst.at[it], s_e.at[it, k], r_e.at[it, k], (mate, lat))

    def outer(it, left, left_mate, right, right_mate, acc, first, second):
        drain(left_mate.at[it], r_e.at[it, first])
        drain(right_mate.at[it], r_e.at[it, second])
        tall = jnp.concatenate([left[it], left_mate[it]], axis=0)
        for j in range(2):
            own = [right[it, 4 * core + 2 * j + h] for h in range(2)]
            other = [right_mate[it, 2 * j + h] for h in range(2)]
            wide = jnp.concatenate(
                [jnp.concatenate(own, axis=1), jnp.concatenate(other, axis=1)], axis=0
            )
            part = lax.dot_general(
                tall, wide, (((0,), (0,)), ((), ())), preferred_element_type=F32
            )
            for h in range(2):
                acc[2 * j + h] += part[:, 128 * h : 128 * (h + 1)].reshape(NX, 2 * NZH, 16, 128)

    def outer_down(it):
        outer(it, mv, mr, hid, hr, accd, 2, 1)

    def outer_up(it):
        outer(it, nn, nr, gp, gr, accu, 0, 3)

    def taps(s):
        def row(i, carry):
            f = pf[i + 1, 8:24]
            for a in range(3):
                for b in range(3):
                    prod = px[s, i + a, 7 + b : 23 + b] * f
                    kacc[3 * a + b] += prod[:8] + prod[8:]
            rows = pl.ds(pl.multiple_of(i * 16, 16), 16)
            prod = gn[rows, :] * nrm[rows, :]
            gacc[...] += prod[:8] + prod[8:]
            return carry

        lax.fori_loop(0, 8, row, 0)

    def spread(it, s, k):
        lanes = pl.ds(128 * k, 128)

        def row(i, carry):
            own = wb[s, 0, i] * gg[i, 0:16, lanes]
            own = own + wb[s, 1, i] * gg[i + 1, 0:16, lanes]
            own = own + wb[s, 2, i] * gg[i, 1:17, lanes]
            own = own + wb[s, 3, i] * gg[i + 1, 1:17, lanes]
            win[it, k, 0, i] = own.astype(BF16)
            return carry

        lax.fori_loop(0, 8, row, 0)
        for d in (2, 1, 3, 4):
            send(
                win.at[it, k, 0], win.at[it, k, d], s_l.at[it, k], r_l.at[it, k],
                at(-2 * d, 0),
            )

    def forward(it, s):
        def row(i, carry):
            u = px[s, i + 1, 8:24]
            running = jnp.zeros_like(u)
            for a in range(3):
                for b in range(3):
                    running = running + kern[a, b : b + 1, :] * (
                        px[s, i + a, 7 + b : 23 + b]
                    )
            u = u + running
            root = lax.rsqrt(jnp.mean(u * u, axis=-1, keepdims=True) + EPSILON)
            rows = pl.ds(pl.multiple_of(i * 16, 16), 16)
            normed = u * root
            nrm[rows, :] = normed
            inv[rows, :] = jnp.broadcast_to(root, (16, 128))
            nn[it, rows, :] = (normed * gain[...]).astype(BF16)
            return carry

        lax.fori_loop(0, 8, row, 0)
        exchange(nn.at[it], nr, it, 0)

        def block(j, carry):
            cols = pl.ds(pl.multiple_of(j * 256, 256), 256)
            pre = jnp.dot(nn[it], wu[:, cols], preferred_element_type=F32)
            sig = jax.nn.sigmoid(pre)
            hidden = (pre * sig).astype(BF16)
            slope = sig * (1.0 + pre * (1.0 - sig))
            for h in range(2):
                hid[it, 2 * j + h] = hidden[:, 128 * h : 128 * (h + 1)]
                ds[2 * j + h] = slope[:, 128 * h : 128 * (h + 1)]
            return carry

        lax.fori_loop(0, 4, block, 0)
        exchange(hid.at[it, pl.ds(4 - 4 * core, 4)], hr, it, 1)

    def transport(it, s):
        def arrive(g):
            drain(win.at[it, g, 1 : AHEAD + 1], r_l.at[it, g])
            for d in range(AHEAD + 1):
                near_by[g, d] = win[it, g, d]
            far = lax.div(lm[s, g], 8)
            ps[it, g] = near_by[g, lax.div(far, 2) + 1 - core]
            send(ps.at[it, g], pr.at[it, g], s_p.at[it, g], r_p.at[it, g], (mate, lat))

        def along(g):
            drain(pr.at[it, g], r_p.at[it, g])
            move = lm[s, g]
            far = lax.div(move, 8)
            odd = pr[it, g]
            lon2[g, 0:8] = odd
            lon2[g, 8:16] = near_by[g, lax.div(far + 1, 2)]
            lon2[g, 16:24] = odd
            begin = 8 - 8 * lax.rem(far, 2) + lax.rem(move, 8)
            for i in range(8):
                own = lon2[g, begin + i]
                lb[it, g, i] = own
                lwin[g, i, 0:16] = own
            for d in (2, 1):
                send(
                    lb.at[it, g], lw.at[it, g, d - 1], s_t.at[it, g], r_t.at[it, g], at(0, -d)
                )

        def settle(g):
            drain(lw.at[it, g], r_t.at[it, g])
            lwin[g, :, 16:32] = cut(lat < LAT - 1, lw[it, g, 0])
            lwin[g, :, 32:48] = cut(lat < LAT - 2, lw[it, g, 1])
            pick = jnp.where(diff[...] == lt[s, g], 1.0, 0.0).astype(BF16)
            mv[it, :, 128 * g : 128 * (g + 1)] = jnp.dot(
                pick, lwin[g].reshape(8 * 48, 128), preferred_element_type=F32
            ).astype(BF16)

        for g in range(GROUPS):
            arrive(g)
            if g >= 2:
                settle(g - 2)
            along(g)
        settle(GROUPS - 2)
        settle(GROUPS - 1)

    def backward(it):
        exchange(mv.at[it], mr, it, 2)
        total = None
        for turn in range(4):
            j = lax.rem(2 - 2 * core + turn, 4)
            cols = pl.ds(pl.multiple_of(j * 256, 256), 256)
            up = jnp.dot(mv[it], wd[:, cols], preferred_element_type=F32)
            slope = jnp.concatenate([ds[2 * j], ds[2 * j + 1]], axis=1)
            pre = (up * slope).astype(BF16)
            gp[it, 2 * j] = pre[:, :128]
            gp[it, 2 * j + 1] = pre[:, 128:]
            if turn == 1:
                exchange(gp.at[it, pl.ds(4 - 4 * core, 4)], gr, it, 3)
            part = lax.dot_general(
                pre, wu[:, cols], (((1,), (1,)), ((), ())), preferred_element_type=F32
            )
            total = part if total is None else total + part
        gn[...] = total

        def row(i, carry):
            rows = pl.ds(pl.multiple_of(i * 16, 16), 16)
            normed = nrm[rows, :]
            scaled = gn[rows, :] * gain[...]
            mean = jnp.mean(scaled * normed, axis=-1, keepdims=True)
            root = jnp.concatenate([inv[rows, :]] * GROUPS, axis=1)
            field = (mv[it, rows, :].astype(F32) + root * (scaled - normed * mean)).astype(BF16)
            fld[it + 1, i] = field
            pf[i + 1, 8:24] = field.astype(F32)
            return carry

        lax.fori_loop(0, 8, row, 0)

    halo_send(0)
    for k, (a, b) in enumerate(((-1, 0), (0, -1), (-1, -1))):
        send(bt, br.at[k], s_bt.at[k], r_bt, at(a, b))
    state_edges = [
        (st.at[:, 7], at(1, 0)), (st.at[:, 0], at(-1, 0)), (sxs, at(0, 1)), (sxs, at(0, -1)),
        (sxs, at(1, 1)), (sxs, at(1, -1)), (sxs, at(-1, 1)), (sxs, at(-1, -1)),
    ]
    for k, (src, target) in enumerate(state_edges):
        send(src, sxr.at[k], s_sx.at[k], r_sx, target)

    accu[...] = jnp.zeros_like(accu)
    accd[...] = jnp.zeros_like(accd)
    kacc[...] = jnp.zeros_like(kacc)
    gacc[...] = jnp.zeros_like(gacc)

    drain(br, r_bt)
    pt[0, 0:16] = bt[...]
    pt[0, 16:17] = cut(not_high, br[1, 0:1])
    pt[1, 0:16] = br[0]
    pt[1, 16:17] = cut(not_high, br[2, 0:1])
    for i in range(8):
        for q, (di, dj) in enumerate(((0, 0), (1, 0), (0, 1), (1, 1))):
            rows = pt[(i + di) // 8, dj : dj + 16]
            for s in range(STEPS):
                lane = (4 * s + q) * 8 + (i + di) % 8
                wb[s, q, i] = jnp.broadcast_to(rows[:, lane : lane + 1], (16, 128))

    def fill_states():
        drain(sxr, r_sx)
        for s in range(STEPS):
            edge = [sxr[k, s].astype(F32) for k in range(8)]
            px[s, 0, 8:24] = edge[0]
            px[s, 9, 8:24] = edge[1]
            lo, hi = cut(not_low, edge[2]), cut(not_high, edge[3])
            put_column(px.at[s], 7, lo[8:16])
            put_column(px.at[s], 24, hi[0:8])
            px[s, 0, 7:8] = cut(not_low, edge[4])[15:16]
            px[s, 0, 24:25] = cut(not_high, edge[5])[7:8]
            px[s, 9, 7:8] = cut(not_low, edge[6])[8:9]
            px[s, 9, 24:25] = cut(not_high, edge[7])[0:1]

    for copy in fetch:
        copy.wait()

    def step(it, carry):
        s = STEPS - 1 - it

        @pl.when(it > 0)
        def _():
            halo_send(it)
            outer_down(it - 1)
            outer_up(it - 1)
            taps(s + 1)

        halo_fill(it)
        for k in range(GROUPS):
            stencil(it, 9, k)
            spread(it, s, k)
        pl.when(it == 0)(fill_states)
        forward(it, s)
        transport(it, s)
        backward(it)
        return carry

    lax.fori_loop(0, STEPS, step, 0)
    halo_send(STEPS)

    outer_down(STEPS - 1)
    b1d[...] = accd[...].astype(BF16)
    for d in range(1, NX):
        send(b1d.at[:, lax.rem(xx + d, NX)], rxd.at[d - 1], s_x.at[0, d - 1], r_x.at[0], at_x(d))
    outer_up(STEPS - 1)
    b1u[...] = accu[...].astype(BF16)
    for d in range(1, NY):
        send(b1u.at[lax.rem(yy + d, NY)], ryu.at[d - 1], s_y.at[1, d - 1], r_y.at[1], at_y(d))

    taps(0)

    sums = [jnp.sum(kacc[k], axis=0, keepdims=True) for k in range(9)]
    sums.append(jnp.sum(gacc[...], axis=0, keepdims=True))
    table = jnp.concatenate(sums, axis=0)
    for k in range(GROUPS):
        smc[core, 8 * k : 8 * k + 8, :] = table[0:8, 128 * k : 128 * (k + 1)]
        smc[core, 32 + 2 * k : 34 + 2 * k, :] = table[8:10, 128 * k : 128 * (k + 1)]
    send(smc.at[core], smc.at[core], s_sm.at[0], r_sm.at[0], (mate, lat))

    drain(smc.at[0], r_sm.at[0])
    smy[yy] = smc[0] + smc[1]
    for d in range(1, NY):
        send(smy.at[yy], smy.at[yy], s_sm.at[d], r_sm.at[1], at_y(d))

    halo_fill(STEPS)
    for k in range(GROUPS):
        stencil(STEPS, 8, k)
    for i in range(8):
        gs_out[i] = gg[i, 0:16].astype(BF16)

    drain(smy.at[0:3], r_sm.at[1])
    smx[xx] = ((smy[0] + smy[1]) + smy[2]) + smy[3]
    for d in range(1, NX):
        send(smx.at[xx], smx.at[xx], s_sm.at[3 + d], r_sm.at[2], at_x(d))

    drain(rxd, r_x.at[0])
    total = accd[:, xx]
    for d in range(NX - 1):
        total = total + rxd[d].astype(F32)
    b2d[...] = total.astype(BF16)
    for d in range(1, NY):
        send(b2d.at[lax.rem(yy + d, NY)], ryd.at[d - 1], s_y.at[0, d - 1], r_y.at[0], at_y(d))

    drain(ryu, r_y.at[1])
    total = accu[yy]
    for d in range(NY - 1):
        total = total + ryu[d].astype(F32)
    b2u[...] = total.astype(BF16)
    for d in range(1, NX):
        send(b2u.at[lax.rem(xx + d, NX)], rxu.at[d - 1], s_x.at[1, d - 1], r_x.at[1], at_x(d))

    drain(smx.at[0:3], r_sm.at[2])
    here = zl * NZH + zh
    smz[here] = ((smx[0] + smx[1]) + smx[2]) + smx[3]
    for k, (dzl, dzh) in enumerate(zpairs):
        send(smz.at[here], smz.at[here], s_sm.at[7 + k], r_sm.at[3], at_z(dzl, dzh))

    mine = zh * 2 + zl
    alone = zl == core
    for m, r2, own, b3, rz, rsem in (
        (0, ryd, b2d.at[yy], b3d, rzd, r_y.at[0]), (1, rxu, b2u.at[xx], b3u, rzu, r_x.at[1])
    ):
        drain(r2, rsem)
        total = own[...].astype(F32)
        for d in range(3):
            total = total + r2[d].astype(F32)
        b3[...] = total.astype(BF16)
        for k in range(8):
            to_zh, to_core = lax.rem(zh + k // 2, NZH), lax.rem(core + k % 2, 2)
            piece = b3.at[to_zh * 2 + to_core]
            target = ((xx * NZH + to_zh) * 2 + to_core, core * NY + yy)

            def remote(piece=piece, rz=rz, m=m, k=k, target=target):
                send(piece, rz.at[mine], s_z.at[m, k], r_z.at[m], target)

            if k:
                remote()
            else:
                pl.when(jnp.logical_not(alone))(remote)

                @pl.when(alone)
                def _(b3=b3, rz=rz):
                    rz[mine] = b3[zh * 2 + core]

    drain(smz.at[0:7], r_sm.at[3])
    total = smz[0]
    for k in range(1, 8):
        total = total + smz[k]
    for k in range(GROUPS):
        for tap in range(9):
            at_row = 8 * k + tap if tap < 8 else 32 + 2 * k
            kern_out[tap // 3, tap % 3 : tap % 3 + 1, 128 * k : 128 * (k + 1)] = (
                total[at_row : at_row + 1]
            )
        gain_out[:, 128 * k : 128 * (k + 1)] = total[33 + 2 * k : 34 + 2 * k]

    for m, rz, out in ((0, rzd, dn_out), (1, rzu, up_out)):

        @pl.when(alone)
        def _(rz=rz, m=m):
            drain(rz.at[0:7], r_z.at[m])

        @pl.when(jnp.logical_not(alone))
        def _(rz=rz, m=m):
            drain(rz, r_z.at[m])

        total = rz[0].astype(F32)
        for k in range(1, 8):
            total = total + rz[k].astype(F32)
        out[...] = total

    for k in range(8):
        drain(sxs, s_sx.at[k])
    for k in range(3):
        drain(bt, s_bt.at[k])

    def sent(it, carry):
        halo_sent(it)
        for g in range(GROUPS):
            drain(win.at[it, g, 1 : AHEAD + 1], s_l.at[it, g])
            drain(ps.at[it, g], s_p.at[it, g])
            drain(lw.at[it, g], s_t.at[it, g])
        for k, ref in enumerate((nr, hr, mr, gr)):
            drain(ref.at[it], s_e.at[it, k])
        return carry

    lax.fori_loop(0, STEPS, sent, 0)
    halo_sent(STEPS)
    for m in range(2):
        for k in range(1, 8):
            drain(b3u.at[0], s_z.at[m, k])

        @pl.when(jnp.logical_not(alone))
        def _(m=m):
            drain(b3u.at[0], s_z.at[m, 0])

    for d in range(3):
        drain(rxd.at[0], s_x.at[0, d])
        drain(rxu.at[0], s_x.at[1, d])
        drain(ryd.at[0], s_y.at[0, d])
        drain(ryu.at[0], s_y.at[1, d])
    for k in range(14):
        drain(smc.at[0], s_sm.at[k])


def hand_over(*refs):
    for source, result in zip(refs[:5], refs[5:]):
        result[...] = source[...]


def local(cotangent, states, w_up, w_down, norm_gain, kernel_taps, bilinear, lon_move, lat_move):
    vm, sm = pltpu.VMEM, pltpu.SemaphoreType.DMA
    scratch = [
        vm((512, 1024), BF16),
        vm((512, 1024), BF16),
        vm((STEPS, 10, PW, 512), F32),
        vm((11, PW, 512), F32),
        vm((9, GW, 512), F32),
        vm((STEPS, 4, 8, 16, 128), F32),
        vm((128, 128), F32),
        vm((16, 128), F32),
        vm((2, GW, 128), F32),
        vm((STEPS + 1, 8, 16, 512), BF16),
        vm((STEPS + 1, 2, 16, 512), BF16),
        vm((STEPS + 1, 9, 16, 512), BF16),
        vm((STEPS, 16, 512), BF16),
        vm((8, STEPS, 16, 512), BF16),
        vm((3, 16, 128), F32),
        vm((STEPS, GROUPS, AHEAD + 1, 8, 16, 128), BF16),
        vm((GROUPS, AHEAD + 1, 8, 16, 128), BF16),
        vm((STEPS, GROUPS, 8, 16, 128), BF16),
        vm((STEPS, GROUPS, 8, 16, 128), BF16),
        vm((GROUPS, 24, 16, 128), BF16),
        vm((STEPS, GROUPS, 8, 16, 128), BF16),
        vm((STEPS, GROUPS, 2, 8, 16, 128), BF16),
        vm((GROUPS, 8, 48, 128), BF16),
        vm((128, 8 * 48), jnp.int32),
        vm((STEPS, 128, 512), BF16),
        vm((STEPS, 128, 512), BF16),
        vm((STEPS, 128, 512), BF16),
        vm((STEPS, 128, 512), BF16),
        vm((STEPS, 8, 128, 128), BF16),
        vm((STEPS, 4, 128, 128), BF16),
        vm((STEPS, 8, 128, 128), BF16),
        vm((STEPS, 4, 128, 128), BF16),
        vm((8, 128, 128), F32),
        vm((128, 512), F32),
        vm((128, 128), F32),
        vm((128, 512), F32),
        vm((NY, NX, 2 * NZH, 16, 128), F32),
        vm((NY, NX, 2 * NZH, 16, 128), F32),
        vm((9, 8, 512), F32),
        vm((8, 512), F32),
        vm((NY, NX, 2 * NZH, 16, 128), BF16),
        vm((3, NX, 2 * NZH, 16, 128), BF16),
        vm((NX, 2 * NZH, 16, 128), BF16),
        vm((3, 2 * NZH, 16, 128), BF16),
        vm((2 * NZH, 16, 128), BF16),
        vm((8, 16, 128), BF16),
        vm((NY, NX, 2 * NZH, 16, 128), BF16),
        vm((3, NY, 2 * NZH, 16, 128), BF16),
        vm((NY, 2 * NZH, 16, 128), BF16),
        vm((3, 2 * NZH, 16, 128), BF16),
        vm((2 * NZH, 16, 128), BF16),
        vm((8, 16, 128), BF16),
        vm((2, 40, 128), F32),
        vm((NY, 40, 128), F32),
        vm((NX, 40, 128), F32),
        vm((NZL * NZH, 40, 128), F32),
        sm((2,)), sm((8,)), sm, sm((3,)), sm,
        sm((STEPS + 1, 8)), sm((STEPS + 1,)),
        sm((STEPS, GROUPS)), sm((STEPS, GROUPS)),
        sm((STEPS, GROUPS)), sm((STEPS, GROUPS)),
        sm((STEPS, GROUPS)), sm((STEPS, GROUPS)),
        sm((STEPS, 4)), sm((STEPS, 4)),
        sm((2, 3)), sm((2,)), sm((2, 3)), sm((2,)), sm((2, 8)), sm((2,)),
        sm((14,)), sm((4,)),
    ]
    vmem = pl.BlockSpec(memory_space=pltpu.VMEM)
    smem = pl.BlockSpec(memory_space=pltpu.SMEM)
    anywhere = pl.BlockSpec(memory_space=pl.ANY)
    swept = pl.pallas_call(
        kernel,
        out_shape=(
            jax.ShapeDtypeStruct((8, 16, 512), BF16),
            jax.ShapeDtypeStruct((16, 128), F32),
            jax.ShapeDtypeStruct((16, 128), F32),
            jax.ShapeDtypeStruct((3, 3, 512), F32),
            jax.ShapeDtypeStruct((1, 512), F32),
        ),
        in_specs=[vmem] * 2 + [anywhere] * 2 + [vmem] * 3 + [smem] * 2,
        out_specs=(vmem,) * 5,
        scratch_shapes=scratch,
        compiler_params=pltpu.CompilerParams(
            collective_id=0, has_side_effects=True, vmem_limit_bytes=56 * 1024 * 1024
        ),
    )(
        cotangent, states, w_up, w_down, norm_gain.reshape(1, 512),
        kernel_taps, bilinear, lon_move, lat_move,
    )
    grad_state, grad_up, grad_down, grad_kernel, grad_gain = pl.pallas_call(
        hand_over,
        out_shape=tuple(jax.ShapeDtypeStruct(a.shape, a.dtype) for a in swept),
        in_specs=[vmem] * 5,
        out_specs=(vmem,) * 5,
    )(*swept)
    return (grad_state, grad_up, grad_down, grad_kernel, grad_gain.reshape(512))


def solution(mesh):
    placed = (
        P("lon", "lat", None),
        P(None, "lon", "lat", None),
        P(),
        P(),
        P(),
        P(),
        P(None, None, "lon", "lat"),
        P(),
        P(),
    )
    return jax.shard_map(
        local,
        mesh=mesh,
        in_specs=placed,
        out_specs=(P("lon", "lat", None), P("lon", "lat"), P("lon", "lat"), P(), P()),
        check_vma=False,
    )
```

```python
import jax
import jax.numpy as jnp
from jax import lax
from jax.experimental import pallas as pl
from jax.experimental.pallas import tpu as pltpu
from jax.sharding import PartitionSpec as P

GROUPS = 4
STEPS = 3
EPSILON = 1e-06
MESH = pl.DeviceIdType.MESH
F32 = jnp.float32
BF16 = jnp.bfloat16

NX, NZH, NZL, NY = 4, 4, 2, 4
LON, LAT = NX * NZH * 2, NZL * NY
AHEAD = 4
PW = 32
FW = 72
WIDE = 3
GW = 24


def kernel(
    cot, st, wu_hbm, wd_hbm, gain, kern, bil, lm, lt,
    gs_out, up_out, dn_out, kern_out, gain_out,
    wu, wd, px, pf, gg, wb, square, bt, pt, fld, stg, stl, hl, hh, hp, hn, sxs, sxl, sxc, br,
    win, near_by, ps, pr, lon2, lw, lwin, diff,
    mv, mr, nn, nr, hid, hr, gp, gr, ds, nrm, inv, gn, accu, accd, kacc, gacc,
    b1u, ryu, b2u, rxu, b3u, rzu, b1d, rxd, b2d, ryd, b3d, rzd,
    smc, smy, smx, smz,
    s_w, s_sx, r_sx, s_bt, r_bt, s_hl, s_hh, s_hp, s_hn, r_h, s_l, r_l, s_p, r_p, s_t, r_t,
    s_e, r_e, s_y, r_y, s_x, r_x, s_z, r_z, s_sm, r_sm,
):
    lon = lax.axis_index("lon")
    lat = lax.axis_index("lat")
    core = lax.rem(lon, 2)
    chip = lon // 2
    xx, zh = chip // NZH, lax.rem(chip, NZH)
    zl, yy = lat // NY, lax.rem(lat, NY)
    mate = lon + 1 - 2 * core

    def at(dlon, dlat):
        return (lax.rem(lon + dlon + LON, LON), lax.rem(lat + dlat + LAT, LAT))

    def at_y(d):
        return (lon, zl * NY + lax.rem(yy + d, NY))

    def at_x(d):
        return (lax.rem(xx + d, NX) * (2 * NZH) + zh * 2 + core, lat)

    def at_z(dzl, dzh):
        return (
            (xx * NZH + lax.rem(zh + dzh, NZH)) * 2 + core,
            lax.rem(zl + dzl, NZL) * NY + yy,
        )

    def at_pillar(dzl, dzh, dcore):
        return (
            (xx * NZH + lax.rem(zh + dzh, NZH)) * 2 + lax.rem(core + dcore, 2),
            lax.rem(zl + dzl, NZL) * NY + yy,
        )

    def send(src, dst, ssem, rsem, target):
        pltpu.make_async_remote_copy(
            src_ref=src, dst_ref=dst, send_sem=ssem, recv_sem=rsem,
            device_id=target, device_id_type=MESH,
        ).start()

    def drain(ref, sem):
        pltpu.make_async_copy(ref, ref, sem).wait()

    near = [(a, b) for a in (-1, 0, 1) for b in range(-WIDE, WIDE + 1) if (a, b) != (0, 0)]
    zpairs = [(a, b) for a in range(NZL) for b in range(NZH) if (a, b) != (0, 0)]
    pillar = [(a, b, c) for a in range(NZL) for b in range(NZH) for c in range(2) if a + b + c]
    partners = [at(a, b) for a, b in near]
    partners += [at(2 * d * sign, 0) for d in range(1, AHEAD + 1) for sign in (-1, 1)]
    partners += [at_y(d) for d in range(1, NY)] + [at_x(d) for d in range(1, NX)]
    partners += [at_pillar(a, b, c) for a, b, c in pillar]
    barrier = pltpu.get_barrier_semaphore()
    for target in partners:
        pl.semaphore_signal(barrier, inc=1, device_id=target, device_id_type=MESH)

    def column(ref, j):
        return [ref[i, j : j + 1] for i in range(1, 9)]

    def put_column(ref, j, rows):
        for i in range(8):
            ref[i + 1, j : j + 1] = rows[i : i + 1]

    fetch = [
        pltpu.make_async_copy(wu_hbm, wu, s_w.at[0]), pltpu.make_async_copy(wd_hbm, wd, s_w.at[1])
    ]
    for copy in fetch:
        copy.start()

    not_low = lat > 0
    not_high = lat < LAT - 1
    for i in range(8):
        block = cot[i]
        fld[0, i] = block
        pf[i + 1, 8:24] = block.astype(F32)
        for s in range(STEPS):
            px[s, i + 1, 8:24] = st[s, i].astype(F32)
    for s in range(STEPS):
        for k, j in enumerate((8, 23)):
            sxs[s, k] = jnp.concatenate(column(px.at[s], j), axis=0).astype(BF16)
    square[...] = jnp.zeros_like(square)
    square[0 : 32 * STEPS, 0:16] = bil[...].reshape(32 * STEPS, 16)
    bt[...] = jnp.transpose(square[...])[0:16]
    place = lax.broadcasted_iota(jnp.int32, diff.shape, 0)
    diff[...] = (
        lax.broadcasted_iota(jnp.int32, diff.shape, 1)
        - lax.div(place, 16) * 48 - lax.rem(place, 16)
    )
    pl.semaphore_wait(barrier, len(partners))

    def halo_send(it, tiles):
        first, second, last = column(pf, 8), column(pf, 9), column(pf, 23)
        stg[it] = jnp.concatenate(first + second, axis=0).astype(BF16)
        stl[it] = jnp.concatenate(last, axis=0).astype(BF16)
        for k, a in enumerate((-1, 0, 1)):
            send(stl.at[it], hl.at[it, k], s_hl.at[it, k], r_h.at[it, 0], at(-a, 1))
            send(stg.at[it], hh.at[it, k], s_hh.at[it, k], r_h.at[it, 1], at(-a, -tiles))
        for t in range(tiles):
            send(fld.at[it, 7], hp.at[it, t], s_hp.at[it, t], r_h.at[it, 2], at(1, -t))
            send(fld.at[it, 0:2], hn.at[it, t], s_hn.at[it, t], r_h.at[it, 3], at(-1, -t))
        if tiles == WIDE:
            for g in range(GROUPS):
                for t in (2, 1):
                    send(
                        fld.at[it, :, :, pl.ds(128 * g, 128)], lw.at[it, g, t - 1],
                        s_t.at[it, g], r_t.at[it, g], at(0, -t),
                    )

    def halo_sent(it, tiles):
        for k in range(3):
            drain(stl.at[it], s_hl.at[it, k])
            drain(stg.at[it], s_hh.at[it, k])
        for t in range(tiles):
            drain(fld.at[it, 7], s_hp.at[it, t])
            drain(fld.at[it, 0:2], s_hn.at[it, t])

    def cut(keep, value):
        return jnp.where(keep, value, jnp.zeros_like(value))

    def halo_fill(it, tiles):
        drain(hl.at[it], r_h.at[it, 0])
        drain(hh.at[it], r_h.at[it, 1])
        drain(hp.at[it, 0:tiles], r_h.at[it, 2])
        drain(hn.at[it, 0:tiles], r_h.at[it, 3])
        for t in range(tiles):
            inside = lat < LAT - t
            cols = slice(8 + 16 * t, 24 + 16 * t)
            pf[0, cols] = cut(inside, hp[it, t].astype(F32))
            pf[9, cols] = cut(inside, hn[it, t, 0].astype(F32))
            pf[10, cols] = cut(inside, hn[it, t, 1].astype(F32))
        end = 8 + 16 * tiles
        lo = [cut(not_low, hl[it, k].astype(F32)) for k in range(3)]
        hi = [cut(lat < LAT - tiles, hh[it, k].astype(F32)) for k in range(3)]
        put_column(pf, 7, lo[1])
        put_column(pf, end, hi[1][0:8])
        put_column(pf, end + 1, hi[1][8:16])
        pf[0, 7:8] = lo[0][7:8]
        pf[0, end : end + 1] = hi[0][7:8]
        pf[0, end + 1 : end + 2] = hi[0][15:16]
        for r in (0, 1):
            pf[9 + r, 7:8] = lo[2][r : r + 1]
            pf[9 + r, end : end + 1] = hi[2][r : r + 1]
            pf[9 + r, end + 1 : end + 2] = hi[2][8 + r : 9 + r]

    def tiles_fill(it, g):
        drain(lw.at[it, g], r_t.at[it, g])
        for t in (1, 2):
            for i in range(8):
                pf[i + 1, 8 + 16 * t : 24 + 16 * t, 128 * g : 128 * (g + 1)] = cut(
                    lat < LAT - t, lw[it, g, t - 1, i].astype(F32)
                )

    def stencil(it, rows, k, t):
        on = jnp.where(it > 0, 1.0, 0.0).astype(F32)
        base = 8 + 16 * t
        lanes = pl.ds(128 * k, 128)

        def row(i, carry):
            centre = pf[i + 1, base : base + GW - 2, lanes]
            running = jnp.zeros_like(centre)
            for a in range(3):
                for b in range(3):
                    tap = kern[a, b : b + 1, lanes] * on
                    running = running + tap * (
                        pf[i + 2 - a, base + 1 - b : base + 1 - b + GW - 2, lanes]
                    )
            gg[i, 0 : GW - 2, lanes] = (centre + running).astype(BF16).astype(F32)
            return carry

        lax.fori_loop(0, rows, row, 0, unroll=3 if rows == 9 else 4)

    def exchange(src, dst, it, k):
        send(src, dst.at[it], s_e.at[it, k], r_e.at[it, k], (mate, lat))

    def outer(it, left, left_mate, right, right_mate, acc, first, second):
        drain(left_mate.at[it], r_e.at[it, first])
        drain(right_mate.at[it], r_e.at[it, second])
        tall = jnp.concatenate([left[it], left_mate[it]], axis=0)
        for j in range(2):
            own = [right[it, 4 * core + 2 * j + h] for h in range(2)]
            other = [right_mate[it, 2 * j + h] for h in range(2)]
            wide = jnp.concatenate(
                [jnp.concatenate(own, axis=1), jnp.concatenate(other, axis=1)], axis=0
            )
            part = lax.dot_general(
                tall, wide, (((0,), (0,)), ((), ())), preferred_element_type=F32
            )
            for h in range(2):
                acc[2 * j + h] += part[:, 128 * h : 128 * (h + 1)].reshape(NX, 2 * NZH, 16, 128)

    def outer_down(it):
        outer(it, mv, mr, hid, hr, accd, 2, 1)

    def outer_up(it):
        outer(it, nn, nr, gp, gr, accu, 0, 3)

    def taps(s):
        def row(i, carry):
            f = pf[i + 1, 8:24]
            for a in range(3):
                for b in range(3):
                    prod = px[s, i + a, 7 + b : 23 + b] * f
                    kacc[3 * a + b] += prod[:8] + prod[8:]
            rows = pl.ds(pl.multiple_of(i * 16, 16), 16)
            prod = gn[rows, :] * nrm[rows, :]
            gacc[...] += prod[:8] + prod[8:]
            return carry

        lax.fori_loop(0, 8, row, 0)

    def spread(s, k, t):
        lanes = pl.ds(128 * k, 128)

        def row(i, carry):
            own = wb[s, 0, t, i] * gg[i, 0:16, lanes]
            own = own + wb[s, 1, t, i] * gg[i + 1, 0:16, lanes]
            own = own + wb[s, 2, t, i] * gg[i, 1:17, lanes]
            own = own + wb[s, 3, t, i] * gg[i + 1, 1:17, lanes]
            lwin[k, i, 16 * t : 16 * t + 16] = own.astype(BF16)
            return carry

        lax.fori_loop(0, 8, row, 0, unroll=4)

    def along_lat(it, s, k):
        pick = jnp.where(diff[...] == lt[s, k], 1.0, 0.0).astype(BF16)
        win[it, k, 0] = jnp.dot(
            pick, lwin[k].reshape(8 * 48, 128), preferred_element_type=F32
        ).astype(BF16).reshape(8, 16, 128)
        for d in (2, 1, 3, 4):
            send(
                win.at[it, k, 0], win.at[it, k, d], s_l.at[it, k], r_l.at[it, k],
                at(-2 * d, 0),
            )

    def forward(it, s):
        def row(i, carry):
            u = px[s, i + 1, 8:24]
            running = jnp.zeros_like(u)
            for a in range(3):
                for b in range(3):
                    running = running + kern[a, b : b + 1, :] * (
                        px[s, i + a, 7 + b : 23 + b]
                    )
            u = u + running
            root = lax.rsqrt(jnp.mean(u * u, axis=-1, keepdims=True) + EPSILON)
            rows = pl.ds(pl.multiple_of(i * 16, 16), 16)
            normed = u * root
            nrm[rows, :] = normed
            inv[rows, :] = jnp.broadcast_to(root, (16, 128))
            nn[it, rows, :] = (normed * gain[...]).astype(BF16)
            return carry

        lax.fori_loop(0, 8, row, 0)
        exchange(nn.at[it], nr, it, 0)

        def block(j, carry):
            cols = pl.ds(pl.multiple_of(j * 256, 256), 256)
            pre = jnp.dot(nn[it], wu[:, cols], preferred_element_type=F32)
            sig = jax.nn.sigmoid(pre)
            hidden = (pre * sig).astype(BF16)
            slope = sig * (1.0 + pre * (1.0 - sig))
            for h in range(2):
                hid[it, 2 * j + h] = hidden[:, 128 * h : 128 * (h + 1)]
                ds[2 * j + h] = slope[:, 128 * h : 128 * (h + 1)]
            return carry

        lax.fori_loop(0, 4, block, 0)
        exchange(hid.at[it, pl.ds(4 - 4 * core, 4)], hr, it, 1)

    def transport(it, s):
        def arrive(g):
            drain(win.at[it, g, 1 : AHEAD + 1], r_l.at[it, g])
            for d in range(AHEAD + 1):
                near_by[g, d] = win[it, g, d]
            far = lax.div(lm[s, g], 8)
            ps[it, g] = near_by[g, lax.div(far, 2) + 1 - core]
            send(ps.at[it, g], pr.at[it, g], s_p.at[it, g], r_p.at[it, g], (mate, lat))

        def along(g):
            drain(pr.at[it, g], r_p.at[it, g])
            move = lm[s, g]
            far = lax.div(move, 8)
            odd = pr[it, g]
            lon2[g, 0:8] = odd
            lon2[g, 8:16] = near_by[g, lax.div(far + 1, 2)]
            lon2[g, 16:24] = odd
            begin = 8 - 8 * lax.rem(far, 2) + lax.rem(move, 8)
            for i in range(8):
                mv[it, 16 * i : 16 * i + 16, 128 * g : 128 * (g + 1)] = lon2[g, begin + i]

        for g in range(GROUPS):
            arrive(g)
            along(g)

    def backward(it):
        exchange(mv.at[it], mr, it, 2)
        total = None
        for turn in range(4):
            j = lax.rem(2 - 2 * core + turn, 4)
            cols = pl.ds(pl.multiple_of(j * 256, 256), 256)
            up = jnp.dot(mv[it], wd[:, cols], preferred_element_type=F32)
            slope = jnp.concatenate([ds[2 * j], ds[2 * j + 1]], axis=1)
            pre = (up * slope).astype(BF16)
            gp[it, 2 * j] = pre[:, :128]
            gp[it, 2 * j + 1] = pre[:, 128:]
            if turn == 1:
                exchange(gp.at[it, pl.ds(4 - 4 * core, 4)], gr, it, 3)
            part = lax.dot_general(
                pre, wu[:, cols], (((1,), (1,)), ((), ())), preferred_element_type=F32
            )
            total = part if total is None else total + part
        gn[...] = total

        def row(i, carry):
            rows = pl.ds(pl.multiple_of(i * 16, 16), 16)
            normed = nrm[rows, :]
            scaled = gn[rows, :] * gain[...]
            mean = jnp.mean(scaled * normed, axis=-1, keepdims=True)
            root = jnp.concatenate([inv[rows, :]] * GROUPS, axis=1)
            field = (mv[it, rows, :].astype(F32) + root * (scaled - normed * mean)).astype(BF16)
            fld[it + 1, i] = field
            pf[i + 1, 8:24] = field.astype(F32)
            return carry

        lax.fori_loop(0, 8, row, 0, unroll=True)

    halo_send(0, WIDE)
    tables = [(a, b) for a in (0, 1) for b in range(WIDE + 1) if a + b]
    for k, (a, b) in enumerate(tables):
        send(bt, br.at[k], s_bt.at[k], r_bt, at(-a, -b))
    state_ways = (at(0, 1), at(0, -1), at(1, 1), at(1, -1), at(-1, 1), at(-1, -1))

    def state_send(s):
        for k, (i, target) in enumerate(((7, at(1, 0)), (0, at(-1, 0)))):
            send(st.at[s, i], sxl.at[s, k], s_sx.at[s, k], r_sx.at[s, 0], target)
        for k, target in enumerate(state_ways):
            side = sxs.at[s, 1 - k % 2]
            send(side, sxc.at[s, k], s_sx.at[s, 2 + k], r_sx.at[s, 1], target)

    state_send(STEPS - 1)

    accu[...] = jnp.zeros_like(accu)
    accd[...] = jnp.zeros_like(accd)
    kacc[...] = jnp.zeros_like(kacc)
    gacc[...] = jnp.zeros_like(gacc)

    drain(br, r_bt)
    pt[0, 0:16] = bt[...]
    for k, (a, b) in enumerate(tables):
        pt[a, 16 * b : 16 * b + 16] = cut(lat < LAT - b, br[k])

    def weights(t, carry):
        for i in range(8):
            for q, (di, dj) in enumerate(((0, 0), (1, 0), (0, 1), (1, 1))):
                from_row = pl.multiple_of(t * 16, 16)
                rows = pt[(i + di) // 8, pl.ds(from_row, 24)][dj : dj + 16]
                for s in range(STEPS):
                    lane = (4 * s + q) * 8 + (i + di) % 8
                    wb[s, q, t, i] = jnp.broadcast_to(rows[:, lane : lane + 1], (16, 128))
        return carry

    lax.fori_loop(0, WIDE, weights, 0)

    def fill_states(s):
        drain(sxl.at[s], r_sx.at[s, 0])
        drain(sxc.at[s], r_sx.at[s, 1])
        px[s, 0, 8:24] = sxl[s, 0].astype(F32)
        px[s, 9, 8:24] = sxl[s, 1].astype(F32)
        edge = [
            cut(not_high if k % 2 else not_low, sxc[s, k].astype(F32)) for k in range(6)
        ]
        put_column(px.at[s], 7, edge[0])
        put_column(px.at[s], 24, edge[1])
        px[s, 0, 7:8] = edge[2][7:8]
        px[s, 0, 24:25] = edge[3][7:8]
        px[s, 9, 7:8] = edge[4][0:1]
        px[s, 9, 24:25] = edge[5][0:1]

    for copy in fetch:
        copy.wait()

    def step(it, carry):
        s = STEPS - 1 - it

        @pl.when(it > 0)
        def _():
            halo_send(it, WIDE)
            outer_down(it - 1)
            outer_up(it - 1)
            taps(s + 1)

        halo_fill(it, WIDE)
        for k in range(GROUPS):
            tiles_fill(it, k)
            for t in range(WIDE):
                stencil(it, 9, k, t)
                spread(s, k, t)
            along_lat(it, s, k)
        @pl.when(it < STEPS - 1)
        def _():
            state_send(s - 1)

        fill_states(s)
        forward(it, s)
        transport(it, s)
        backward(it)
        return carry

    lax.fori_loop(0, STEPS, step, 0)
    halo_send(STEPS, 1)

    outer_down(STEPS - 1)
    b1d[...] = accd[...].astype(BF16)
    for d in range(1, NX):
        send(b1d.at[:, lax.rem(xx + d, NX)], rxd.at[d - 1], s_x.at[0, d - 1], r_x.at[0], at_x(d))
    outer_up(STEPS - 1)
    b1u[...] = accu[...].astype(BF16)
    for d in range(1, NY):
        send(b1u.at[lax.rem(yy + d, NY)], ryu.at[d - 1], s_y.at[1, d - 1], r_y.at[1], at_y(d))

    taps(0)

    sums = [jnp.sum(kacc[k], axis=0, keepdims=True) for k in range(9)]
    sums.append(jnp.sum(gacc[...], axis=0, keepdims=True))
    table = jnp.concatenate(sums, axis=0)
    for k in range(GROUPS):
        smc[core, 8 * k : 8 * k + 8, :] = table[0:8, 128 * k : 128 * (k + 1)]
        smc[core, 32 + 2 * k : 34 + 2 * k, :] = table[8:10, 128 * k : 128 * (k + 1)]
    send(smc.at[core], smc.at[core], s_sm.at[0], r_sm.at[0], (mate, lat))

    drain(smc.at[0], r_sm.at[0])
    smy[yy] = smc[0] + smc[1]
    for d in range(1, NY):
        send(smy.at[yy], smy.at[yy], s_sm.at[d], r_sm.at[1], at_y(d))

    halo_fill(STEPS, 1)
    for k in range(GROUPS):
        stencil(STEPS, 8, k, 0)
    for i in range(8):
        gs_out[i] = gg[i, 0:16].astype(BF16)

    drain(smy.at[0:3], r_sm.at[1])
    smx[xx] = ((smy[0] + smy[1]) + smy[2]) + smy[3]
    for d in range(1, NX):
        send(smx.at[xx], smx.at[xx], s_sm.at[3 + d], r_sm.at[2], at_x(d))

    drain(rxd, r_x.at[0])
    total = accd[:, xx]
    for d in range(NX - 1):
        total = total + rxd[d].astype(F32)
    b2d[...] = total.astype(BF16)
    for d in range(1, NY):
        send(b2d.at[lax.rem(yy + d, NY)], ryd.at[d - 1], s_y.at[0, d - 1], r_y.at[0], at_y(d))

    drain(ryu, r_y.at[1])
    total = accu[yy]
    for d in range(NY - 1):
        total = total + ryu[d].astype(F32)
    b2u[...] = total.astype(BF16)
    for d in range(1, NX):
        send(b2u.at[lax.rem(xx + d, NX)], rxu.at[d - 1], s_x.at[1, d - 1], r_x.at[1], at_x(d))

    drain(smx.at[0:3], r_sm.at[2])
    here = zl * NZH + zh
    smz[here] = ((smx[0] + smx[1]) + smx[2]) + smx[3]
    for k, (dzl, dzh) in enumerate(zpairs):
        send(smz.at[here], smz.at[here], s_sm.at[7 + k], r_sm.at[3], at_z(dzl, dzh))

    mine = zh * 2 + zl
    alone = zl == core
    for m, r2, own, b3, rz, rsem in (
        (0, ryd, b2d.at[yy], b3d, rzd, r_y.at[0]), (1, rxu, b2u.at[xx], b3u, rzu, r_x.at[1])
    ):
        drain(r2, rsem)
        total = own[...].astype(F32)
        for d in range(3):
            total = total + r2[d].astype(F32)
        b3[...] = total.astype(BF16)
        for k in range(8):
            to_zh, to_core = lax.rem(zh + k // 2, NZH), lax.rem(core + k % 2, 2)
            piece = b3.at[to_zh * 2 + to_core]
            target = ((xx * NZH + to_zh) * 2 + to_core, core * NY + yy)

            def remote(piece=piece, rz=rz, m=m, k=k, target=target):
                send(piece, rz.at[mine], s_z.at[m, k], r_z.at[m], target)

            if k:
                remote()
            else:
                pl.when(jnp.logical_not(alone))(remote)

                @pl.when(alone)
                def _(b3=b3, rz=rz):
                    rz[mine] = b3[zh * 2 + core]

    drain(smz.at[0:7], r_sm.at[3])
    total = smz[0]
    for k in range(1, 8):
        total = total + smz[k]
    for k in range(GROUPS):
        for tap in range(9):
            at_row = 8 * k + tap if tap < 8 else 32 + 2 * k
            kern_out[tap // 3, tap % 3 : tap % 3 + 1, 128 * k : 128 * (k + 1)] = (
                total[at_row : at_row + 1]
            )
        gain_out[:, 128 * k : 128 * (k + 1)] = total[33 + 2 * k : 34 + 2 * k]

    for m, rz, out in ((0, rzd, dn_out), (1, rzu, up_out)):

        @pl.when(alone)
        def _(rz=rz, m=m):
            drain(rz.at[0:7], r_z.at[m])

        @pl.when(jnp.logical_not(alone))
        def _(rz=rz, m=m):
            drain(rz, r_z.at[m])

        total = rz[0].astype(F32)
        for k in range(1, 8):
            total = total + rz[k].astype(F32)
        out[...] = total

    for k in range(len(tables)):
        drain(bt, s_bt.at[k])

    def sent(it, carry):
        for k in range(8):
            drain(st.at[0, 0] if k < 2 else sxs.at[0, 0], s_sx.at[it, k])
        halo_sent(it, WIDE)
        for g in range(GROUPS):
            drain(win.at[it, g, 1 : AHEAD + 1], s_l.at[it, g])
            drain(ps.at[it, g], s_p.at[it, g])
            drain(lw.at[it, g], s_t.at[it, g])
        for k, ref in enumerate((nr, hr, mr, gr)):
            drain(ref.at[it], s_e.at[it, k])
        return carry

    lax.fori_loop(0, STEPS, sent, 0)
    halo_sent(STEPS, 1)
    for m in range(2):
        for k in range(1, 8):
            drain(b3u.at[0], s_z.at[m, k])

        @pl.when(jnp.logical_not(alone))
        def _(m=m):
            drain(b3u.at[0], s_z.at[m, 0])

    for d in range(3):
        drain(rxd.at[0], s_x.at[0, d])
        drain(rxu.at[0], s_x.at[1, d])
        drain(ryd.at[0], s_y.at[0, d])
        drain(ryu.at[0], s_y.at[1, d])
    for k in range(14):
        drain(smc.at[0], s_sm.at[k])


def hand_over(*refs):
    for source, result in zip(refs[:5], refs[5:]):
        result[...] = source[...]


def local(cotangent, states, w_up, w_down, norm_gain, kernel_taps, bilinear, lon_move, lat_move):
    vm, sm = pltpu.VMEM, pltpu.SemaphoreType.DMA
    scratch = [
        vm((512, 1024), BF16),
        vm((512, 1024), BF16),
        vm((STEPS, 10, PW, 512), F32),
        vm((11, FW, 512), F32),
        vm((9, GW, 512), F32),
        vm((STEPS, 4, WIDE, 8, 16, 128), F32),
        vm((128, 128), F32),
        vm((16, 128), F32),
        vm((2, 16 * WIDE + 16, 128), F32),
        vm((STEPS + 1, 8, 16, 512), BF16),
        vm((STEPS + 1, 16, 512), BF16),
        vm((STEPS + 1, 8, 512), BF16),
        vm((STEPS + 1, 3, 8, 512), BF16),
        vm((STEPS + 1, 3, 16, 512), BF16),
        vm((STEPS + 1, WIDE, 16, 512), BF16),
        vm((STEPS + 1, WIDE, 2, 16, 512), BF16),
        vm((STEPS, 2, 8, 512), BF16),
        vm((STEPS, 2, 16, 512), BF16),
        vm((STEPS, 6, 8, 512), BF16),
        vm((2 * WIDE + 1, 16, 128), F32),
        vm((STEPS, GROUPS, AHEAD + 1, 8, 16, 128), BF16),
        vm((GROUPS, AHEAD + 1, 8, 16, 128), BF16),
        vm((STEPS, GROUPS, 8, 16, 128), BF16),
        vm((STEPS, GROUPS, 8, 16, 128), BF16),
        vm((GROUPS, 24, 16, 128), BF16),
        vm((STEPS, GROUPS, 2, 8, 16, 128), BF16),
        vm((GROUPS, 8, 48, 128), BF16),
        vm((128, 8 * 48), jnp.int32),
        vm((STEPS, 128, 512), BF16),
        vm((STEPS, 128, 512), BF16),
        vm((STEPS, 128, 512), BF16),
        vm((STEPS, 128, 512), BF16),
        vm((STEPS, 8, 128, 128), BF16),
        vm((STEPS, 4, 128, 128), BF16),
        vm((STEPS, 8, 128, 128), BF16),
        vm((STEPS, 4, 128, 128), BF16),
        vm((8, 128, 128), F32),
        vm((128, 512), F32),
        vm((128, 128), F32),
        vm((128, 512), F32),
        vm((NY, NX, 2 * NZH, 16, 128), F32),
        vm((NY, NX, 2 * NZH, 16, 128), F32),
        vm((9, 8, 512), F32),
        vm((8, 512), F32),
        vm((NY, NX, 2 * NZH, 16, 128), BF16),
        vm((3, NX, 2 * NZH, 16, 128), BF16),
        vm((NX, 2 * NZH, 16, 128), BF16),
        vm((3, 2 * NZH, 16, 128), BF16),
        vm((2 * NZH, 16, 128), BF16),
        vm((8, 16, 128), BF16),
        vm((NY, NX, 2 * NZH, 16, 128), BF16),
        vm((3, NY, 2 * NZH, 16, 128), BF16),
        vm((NY, 2 * NZH, 16, 128), BF16),
        vm((3, 2 * NZH, 16, 128), BF16),
        vm((2 * NZH, 16, 128), BF16),
        vm((8, 16, 128), BF16),
        vm((2, 40, 128), F32),
        vm((NY, 40, 128), F32),
        vm((NX, 40, 128), F32),
        vm((NZL * NZH, 40, 128), F32),
        sm((2,)), sm((STEPS, 8)), sm((STEPS, 2)), sm((7,)), sm,
        sm((STEPS + 1, 3)), sm((STEPS + 1, 3)), sm((STEPS + 1, 3)), sm((STEPS + 1, 3)),
        sm((STEPS + 1, 4)),
        sm((STEPS, GROUPS)), sm((STEPS, GROUPS)),
        sm((STEPS, GROUPS)), sm((STEPS, GROUPS)),
        sm((STEPS, GROUPS)), sm((STEPS, GROUPS)),
        sm((STEPS, 4)), sm((STEPS, 4)),
        sm((2, 3)), sm((2,)), sm((2, 3)), sm((2,)), sm((2, 8)), sm((2,)),
        sm((14,)), sm((4,)),
    ]
    vmem = pl.BlockSpec(memory_space=pltpu.VMEM)
    smem = pl.BlockSpec(memory_space=pltpu.SMEM)
    anywhere = pl.BlockSpec(memory_space=pl.ANY)
    swept = pl.pallas_call(
        kernel,
        out_shape=(
            jax.ShapeDtypeStruct((8, 16, 512), BF16),
            jax.ShapeDtypeStruct((16, 128), F32),
            jax.ShapeDtypeStruct((16, 128), F32),
            jax.ShapeDtypeStruct((3, 3, 512), F32),
            jax.ShapeDtypeStruct((1, 512), F32),
        ),
        in_specs=[vmem] * 2 + [anywhere] * 2 + [vmem] * 3 + [smem] * 2,
        out_specs=(vmem,) * 5,
        scratch_shapes=scratch,
        compiler_params=pltpu.CompilerParams(
            collective_id=0, has_side_effects=True, vmem_limit_bytes=56 * 1024 * 1024
        ),
    )(
        cotangent, states, w_up, w_down, norm_gain.reshape(1, 512),
        kernel_taps, bilinear, lon_move, lat_move,
    )
    grad_state, grad_up, grad_down, grad_kernel, grad_gain = pl.pallas_call(
        hand_over,
        out_shape=tuple(jax.ShapeDtypeStruct(a.shape, a.dtype) for a in swept),
        in_specs=[vmem] * 5,
        out_specs=(vmem,) * 5,
    )(*swept)
    return (grad_state, grad_up, grad_down, grad_kernel, grad_gain.reshape(512))


def solution(mesh):
    placed = (
        P("lon", "lat", None),
        P(None, "lon", "lat", None),
        P(),
        P(),
        P(),
        P(),
        P(None, None, "lon", "lat"),
        P(),
        P(),
    )
    return jax.shard_map(
        local,
        mesh=mesh,
        in_specs=placed,
        out_specs=(P("lon", "lat", None), P("lon", "lat"), P("lon", "lat"), P(), P()),
        check_vma=False,
    )
```

```python
import jax
import jax.numpy as jnp
from jax import lax
from jax.experimental import pallas as pl
from jax.experimental.pallas import tpu as pltpu
from jax.sharding import PartitionSpec as P

GROUPS = 4
STEPS = 3
EPSILON = 1e-06
MESH = pl.DeviceIdType.MESH
F32 = jnp.float32
BF16 = jnp.bfloat16

NX, NZH, NZL, NY = 4, 4, 2, 4
LON, LAT = NX * NZH * 2, NZL * NY
AHEAD = 4
PW = 32
FW = 72
WIDE = 3
GW = 24


def kernel(
    cot_hbm, st_hbm, wu_hbm, wd_hbm, gain, kern, bil, lm, lt,
    gs_out, up_out, dn_out, kern_out, gain_out,
    cot, st, wu, wd, px, pf, gg, wb, square, bt, pt, fld, stg, stl, stc, hl, hh, hc, hp, hn, sxs, sxl, sxc, br,
    win, near_by, ps, pr, lon2, lw, lwin, diff,
    mv, mr, nn, nr, hid, hr, gp, gr, ds, nrm, inv, gn, accu, accd, kacc, gacc,
    b1u, ryu, b2u, rxu, b3u, rzu, b1d, rxd, b2d, ryd, b3d, rzd,
    smc, smy, smx, smz,
    s_w, s_sx, r_sx, s_bt, r_bt, s_hl, s_hh, s_hp, s_hn, r_h, s_l, r_l, s_p, r_p, s_t, r_t,
    s_e, r_e, s_y, r_y, s_x, r_x, s_z, r_z, s_sm, r_sm,
):
    lon = lax.axis_index("lon")
    lat = lax.axis_index("lat")
    core = lax.rem(lon, 2)
    chip = lon // 2
    xx, zh = chip // NZH, lax.rem(chip, NZH)
    zl, yy = lat // NY, lax.rem(lat, NY)
    mate = lon + 1 - 2 * core

    def at(dlon, dlat):
        return (lax.rem(lon + dlon + LON, LON), lax.rem(lat + dlat + LAT, LAT))

    def at_y(d):
        return (lon, zl * NY + lax.rem(yy + d, NY))

    def at_x(d):
        return (lax.rem(xx + d, NX) * (2 * NZH) + zh * 2 + core, lat)

    def at_z(dzl, dzh):
        return (
            (xx * NZH + lax.rem(zh + dzh, NZH)) * 2 + core,
            lax.rem(zl + dzl, NZL) * NY + yy,
        )

    def at_pillar(dzl, dzh, dcore):
        return (
            (xx * NZH + lax.rem(zh + dzh, NZH)) * 2 + lax.rem(core + dcore, 2),
            lax.rem(zl + dzl, NZL) * NY + yy,
        )

    def send(src, dst, ssem, rsem, target):
        pltpu.make_async_remote_copy(
            src_ref=src, dst_ref=dst, send_sem=ssem, recv_sem=rsem,
            device_id=target, device_id_type=MESH,
        ).start()

    def drain(ref, sem):
        pltpu.make_async_copy(ref, ref, sem).wait()

    near = [(a, b) for a in (-1, 0, 1) for b in range(-WIDE, WIDE + 1) if (a, b) != (0, 0)]
    zpairs = [(a, b) for a in range(NZL) for b in range(NZH) if (a, b) != (0, 0)]
    pillar = [(a, b, c) for a in range(NZL) for b in range(NZH) for c in range(2) if a + b + c]
    partners = [at(a, b) for a, b in near]
    partners += [at(2 * d * sign, 0) for d in range(1, AHEAD + 1) for sign in (-1, 1)]
    partners += [at_y(d) for d in range(1, NY)] + [at_x(d) for d in range(1, NX)]
    partners += [at_pillar(a, b, c) for a, b, c in pillar]
    barrier = pltpu.get_barrier_semaphore()
    for target in partners:
        pl.semaphore_signal(barrier, inc=1, device_id=target, device_id_type=MESH)

    def column(ref, j):
        return [ref[i, j : j + 1] for i in range(1, 9)]

    def put_column(ref, j, rows):
        for i in range(8):
            ref[i + 1, j : j + 1] = rows[i : i + 1]

    fetch = [
        pltpu.make_async_copy(wu_hbm, wu, s_w.at[0]), pltpu.make_async_copy(wd_hbm, wd, s_w.at[1])
    ]
    first = [
        pltpu.make_async_copy(cot_hbm, cot, s_w.at[2]), pltpu.make_async_copy(st_hbm, st, s_w.at[3])
    ]
    for copy in first + fetch:
        copy.start()

    for copy in first:
        copy.wait()
    not_low = lat > 0
    not_high = lat < LAT - 1
    for i in range(8):
        block = cot[i]
        fld[0, i] = block
        pf[i + 1, 8:24] = block.astype(F32)
        for s in range(STEPS):
            px[s, i + 1, 8:24] = st[s, i].astype(F32)
    for s in range(STEPS):
        for k, j in enumerate((8, 23)):
            sxs[s, k] = jnp.concatenate(column(px.at[s], j), axis=0).astype(BF16)
    square[...] = jnp.zeros_like(square)
    square[0 : 32 * STEPS, 0:16] = bil[...].reshape(32 * STEPS, 16)
    bt[...] = jnp.transpose(square[...])[0:16]
    place = lax.broadcasted_iota(jnp.int32, diff.shape, 0)
    diff[...] = (
        lax.broadcasted_iota(jnp.int32, diff.shape, 1)
        - lax.div(place, 16) * 48 - lax.rem(place, 16)
    )
    pl.semaphore_wait(barrier, len(partners))

    def halo_send(it, tiles):
        first, second, last = column(pf, 8), column(pf, 9), column(pf, 23)
        stg[it] = jnp.concatenate(first + second, axis=0).astype(BF16)
        stl[it] = jnp.concatenate(last, axis=0).astype(BF16)
        corners = [first[7], second[7], first[0], first[1], second[0], second[1]]
        stc[it] = jnp.concatenate(corners + first[0:2], axis=0).astype(BF16)
        for k, a in enumerate((-1, 0, 1)):
            send(stl.at[it], hl.at[it, k], s_hl.at[it, k], r_h.at[it, 0], at(-a, 1))
            if a:
                send(
                    stc.at[it], hc.at[it, k // 2], s_hh.at[it, k], r_h.at[it, 4], at(-a, -tiles)
                )
            else:
                send(stg.at[it], hh.at[it], s_hh.at[it, k], r_h.at[it, 1], at(0, -tiles))
        for t in range(tiles):
            send(fld.at[it, 7], hp.at[it, t], s_hp.at[it, t], r_h.at[it, 2], at(1, -t))
            send(fld.at[it, 0:2], hn.at[it, t], s_hn.at[it, t], r_h.at[it, 3], at(-1, -t))
        if tiles == WIDE:
            for g in range(GROUPS):
                for t in (2, 1):
                    send(
                        fld.at[it, :, :, pl.ds(128 * g, 128)], lw.at[it, g, t - 1],
                        s_t.at[it, g], r_t.at[it, g], at(0, -t),
                    )

    def halo_sent(it, tiles):
        for k in range(3):
            drain(stl.at[it], s_hl.at[it, k])
            drain(stg.at[it] if k == 1 else stc.at[it], s_hh.at[it, k])
        for t in range(tiles):
            drain(fld.at[it, 7], s_hp.at[it, t])
            drain(fld.at[it, 0:2], s_hn.at[it, t])

    def cut(keep, value):
        return jnp.where(keep, value, jnp.zeros_like(value))

    def halo_fill(it, tiles):
        drain(hl.at[it], r_h.at[it, 0])
        drain(hh.at[it], r_h.at[it, 1])
        drain(hc.at[it], r_h.at[it, 4])
        drain(hp.at[it, 0:tiles], r_h.at[it, 2])
        drain(hn.at[it, 0:tiles], r_h.at[it, 3])
        for t in range(tiles):
            inside = lat < LAT - t
            cols = slice(8 + 16 * t, 24 + 16 * t)
            pf[0, cols] = cut(inside, hp[it, t].astype(F32))
            pf[9, cols] = cut(inside, hn[it, t, 0].astype(F32))
            pf[10, cols] = cut(inside, hn[it, t, 1].astype(F32))
        end = 8 + 16 * tiles
        lo = [cut(not_low, hl[it, k].astype(F32)) for k in range(3)]
        hi = cut(lat < LAT - tiles, hh[it].astype(F32))
        before, after = [cut(lat < LAT - tiles, hc[it, k].astype(F32)) for k in range(2)]
        put_column(pf, 7, lo[1])
        put_column(pf, end, hi[0:8])
        put_column(pf, end + 1, hi[8:16])
        pf[0, 7:8] = lo[0][7:8]
        pf[0, end : end + 1] = before[0:1]
        pf[0, end + 1 : end + 2] = before[1:2]
        for r in (0, 1):
            pf[9 + r, 7:8] = lo[2][r : r + 1]
            pf[9 + r, end : end + 1] = after[2 + r : 3 + r]
            pf[9 + r, end + 1 : end + 2] = after[4 + r : 5 + r]

    def tiles_fill(it, g):
        drain(lw.at[it, g], r_t.at[it, g])
        for t in (1, 2):
            for i in range(8):
                pf[i + 1, 8 + 16 * t : 24 + 16 * t, 128 * g : 128 * (g + 1)] = cut(
                    lat < LAT - t, lw[it, g, t - 1, i].astype(F32)
                )

    def stencil(it, rows, k, t):
        on = jnp.where(it > 0, 1.0, 0.0).astype(F32)
        base = 8 + 16 * t
        lanes = pl.ds(128 * k, 128)

        def row(i, carry):
            centre = pf[i + 1, base : base + GW - 2, lanes]
            running = jnp.zeros_like(centre)
            for a in range(3):
                for b in range(3):
                    tap = kern[a, b : b + 1, lanes] * on
                    running = running + tap * (
                        pf[i + 2 - a, base + 1 - b : base + 1 - b + GW - 2, lanes]
                    )
            gg[i, 0 : GW - 2, lanes] = (centre + running).astype(BF16).astype(F32)
            return carry

        lax.fori_loop(0, rows, row, 0, unroll=3 if rows == 9 else 4)

    def exchange(src, dst, it, k):
        send(src, dst.at[it], s_e.at[it, k], r_e.at[it, k], (mate, lat))

    def outer(it, left, left_mate, right, right_mate, acc, first, second):
        drain(left_mate.at[it], r_e.at[it, first])
        drain(right_mate.at[it], r_e.at[it, second])
        tall = jnp.concatenate([left[it], left_mate[it]], axis=0)
        for j in range(2):
            own = [right[it, 4 * core + 2 * j + h] for h in range(2)]
            other = [right_mate[it, 2 * j + h] for h in range(2)]
            wide = jnp.concatenate(
                [jnp.concatenate(own, axis=1), jnp.concatenate(other, axis=1)], axis=0
            )
            part = lax.dot_general(
                tall, wide, (((0,), (0,)), ((), ())), preferred_element_type=F32
            )
            for h in range(2):
                acc[2 * j + h] += part[:, 128 * h : 128 * (h + 1)].reshape(NX, 2 * NZH, 16, 128)

    def outer_down(it):
        outer(it, mv, mr, hid, hr, accd, 2, 1)

    def outer_up(it):
        outer(it, nn, nr, gp, gr, accu, 0, 3)

    def taps(s):
        def row(i, carry):
            f = pf[i + 1, 8:24]
            for a in range(3):
                for b in range(3):
                    prod = px[s, i + a, 7 + b : 23 + b] * f
                    kacc[3 * a + b] += prod[:8] + prod[8:]
            rows = pl.ds(pl.multiple_of(i * 16, 16), 16)
            prod = gn[rows, :] * nrm[rows, :]
            gacc[...] += prod[:8] + prod[8:]
            return carry

        lax.fori_loop(0, 8, row, 0)

    def spread(s, k, t):
        lanes = pl.ds(128 * k, 128)

        def row(i, carry):
            own = wb[s, 0, t, i] * gg[i, 0:16, lanes]
            own = own + wb[s, 1, t, i] * gg[i + 1, 0:16, lanes]
            own = own + wb[s, 2, t, i] * gg[i, 1:17, lanes]
            own = own + wb[s, 3, t, i] * gg[i + 1, 1:17, lanes]
            lwin[k, i, 16 * t : 16 * t + 16] = own.astype(BF16)
            return carry

        lax.fori_loop(0, 8, row, 0, unroll=4)

    def along_lat(it, s, k):
        pick = jnp.where(diff[...] == lt[s, k], 1.0, 0.0).astype(BF16)
        win[it, k, 0] = jnp.dot(
            pick, lwin[k].reshape(8 * 48, 128), preferred_element_type=F32
        ).astype(BF16).reshape(8, 16, 128)
        for d in (2, 1, 3, 4):
            send(
                win.at[it, k, 0], win.at[it, k, d], s_l.at[it, k], r_l.at[it, k],
                at(-2 * d, 0),
            )

    def forward(it, s):
        def row(i, carry):
            u = px[s, i + 1, 8:24]
            running = jnp.zeros_like(u)
            for a in range(3):
                for b in range(3):
                    running = running + kern[a, b : b + 1, :] * (
                        px[s, i + a, 7 + b : 23 + b]
                    )
            u = u + running
            root = lax.rsqrt(jnp.mean(u * u, axis=-1, keepdims=True) + EPSILON)
            rows = pl.ds(pl.multiple_of(i * 16, 16), 16)
            normed = u * root
            nrm[rows, :] = normed
            inv[rows, :] = jnp.broadcast_to(root, (16, 128))
            nn[it, rows, :] = (normed * gain[...]).astype(BF16)
            return carry

        lax.fori_loop(0, 8, row, 0)
        exchange(nn.at[it], nr, it, 0)

        def block(j, carry):
            cols = pl.ds(pl.multiple_of(j * 256, 256), 256)
            pre = jnp.dot(nn[it], wu[:, cols], preferred_element_type=F32)
            sig = jax.nn.sigmoid(pre)
            hidden = (pre * sig).astype(BF16)
            slope = sig * (1.0 + pre * (1.0 - sig))
            for h in range(2):
                hid[it, 2 * j + h] = hidden[:, 128 * h : 128 * (h + 1)]
                ds[2 * j + h] = slope[:, 128 * h : 128 * (h + 1)]
            return carry

        lax.fori_loop(0, 4, block, 0)
        exchange(hid.at[it, pl.ds(4 - 4 * core, 4)], hr, it, 1)

    def transport(it, s):
        def arrive(g):
            drain(win.at[it, g, 1 : AHEAD + 1], r_l.at[it, g])
            for d in range(AHEAD + 1):
                near_by[g, d] = win[it, g, d]
            far = lax.div(lm[s, g], 8)
            ps[it, g] = near_by[g, lax.div(far, 2) + 1 - core]
            send(ps.at[it, g], pr.at[it, g], s_p.at[it, g], r_p.at[it, g], (mate, lat))

        def along(g):
            drain(pr.at[it, g], r_p.at[it, g])
            move = lm[s, g]
            far = lax.div(move, 8)
            odd = pr[it, g]
            lon2[g, 0:8] = odd
            lon2[g, 8:16] = near_by[g, lax.div(far + 1, 2)]
            lon2[g, 16:24] = odd
            begin = 8 - 8 * lax.rem(far, 2) + lax.rem(move, 8)
            for i in range(8):
                mv[it, 16 * i : 16 * i + 16, 128 * g : 128 * (g + 1)] = lon2[g, begin + i]

        for g in range(GROUPS):
            arrive(g)
            along(g)

    def backward(it):
        exchange(mv.at[it], mr, it, 2)
        total = None
        for turn in range(4):
            j = lax.rem(2 - 2 * core + turn, 4)
            cols = pl.ds(pl.multiple_of(j * 256, 256), 256)
            up = jnp.dot(mv[it], wd[:, cols], preferred_element_type=F32)
            slope = jnp.concatenate([ds[2 * j], ds[2 * j + 1]], axis=1)
            pre = (up * slope).astype(BF16)
            gp[it, 2 * j] = pre[:, :128]
            gp[it, 2 * j + 1] = pre[:, 128:]
            if turn == 1:
                exchange(gp.at[it, pl.ds(4 - 4 * core, 4)], gr, it, 3)
            part = lax.dot_general(
                pre, wu[:, cols], (((1,), (1,)), ((), ())), preferred_element_type=F32
            )
            total = part if total is None else total + part
        gn[...] = total

        def row(i, carry):
            rows = pl.ds(pl.multiple_of(i * 16, 16), 16)
            normed = nrm[rows, :]
            scaled = gn[rows, :] * gain[...]
            mean = jnp.mean(scaled * normed, axis=-1, keepdims=True)
            root = jnp.concatenate([inv[rows, :]] * GROUPS, axis=1)
            field = (mv[it, rows, :].astype(F32) + root * (scaled - normed * mean)).astype(BF16)
            fld[it + 1, i] = field
            pf[i + 1, 8:24] = field.astype(F32)
            return carry

        lax.fori_loop(0, 8, row, 0, unroll=True)

    halo_send(0, WIDE)
    tables = [(a, b) for a in (0, 1) for b in range(WIDE + 1) if a + b]
    for k, (a, b) in enumerate(tables):
        send(bt, br.at[k], s_bt.at[k], r_bt, at(-a, -b))
    state_ways = (at(0, 1), at(0, -1), at(1, 1), at(1, -1), at(-1, 1), at(-1, -1))

    def state_send(s):
        for k, (i, target) in enumerate(((7, at(1, 0)), (0, at(-1, 0)))):
            send(st.at[s, i], sxl.at[s, k], s_sx.at[s, k], r_sx.at[s, 0], target)
        for k, target in enumerate(state_ways):
            side = sxs.at[s, 1 - k % 2]
            send(side, sxc.at[s, k], s_sx.at[s, 2 + k], r_sx.at[s, 1], target)

    state_send(STEPS - 1)

    accu[...] = jnp.zeros_like(accu)
    accd[...] = jnp.zeros_like(accd)
    kacc[...] = jnp.zeros_like(kacc)
    gacc[...] = jnp.zeros_like(gacc)

    drain(br, r_bt)
    pt[0, 0:16] = bt[...]
    for k, (a, b) in enumerate(tables):
        pt[a, 16 * b : 16 * b + 16] = cut(lat < LAT - b, br[k])

    def weights(t, carry):
        for i in range(8):
            for q, (di, dj) in enumerate(((0, 0), (1, 0), (0, 1), (1, 1))):
                from_row = pl.multiple_of(t * 16, 16)
                rows = pt[(i + di) // 8, pl.ds(from_row, 24)][dj : dj + 16]
                for s in range(STEPS):
                    lane = (4 * s + q) * 8 + (i + di) % 8
                    wb[s, q, t, i] = jnp.broadcast_to(rows[:, lane : lane + 1], (16, 128))
        return carry

    lax.fori_loop(0, WIDE, weights, 0)

    def fill_states(s):
        drain(sxl.at[s], r_sx.at[s, 0])
        drain(sxc.at[s], r_sx.at[s, 1])
        px[s, 0, 8:24] = sxl[s, 0].astype(F32)
        px[s, 9, 8:24] = sxl[s, 1].astype(F32)
        edge = [
            cut(not_high if k % 2 else not_low, sxc[s, k].astype(F32)) for k in range(6)
        ]
        put_column(px.at[s], 7, edge[0])
        put_column(px.at[s], 24, edge[1])
        px[s, 0, 7:8] = edge[2][7:8]
        px[s, 0, 24:25] = edge[3][7:8]
        px[s, 9, 7:8] = edge[4][0:1]
        px[s, 9, 24:25] = edge[5][0:1]

    for copy in fetch:
        copy.wait()

    def step(it, carry):
        s = STEPS - 1 - it

        @pl.when(it > 0)
        def _():
            halo_send(it, WIDE)
            outer_down(it - 1)
            outer_up(it - 1)
            taps(s + 1)

        halo_fill(it, WIDE)
        for k in range(GROUPS):
            tiles_fill(it, k)
            for t in range(WIDE):
                stencil(it, 9, k, t)
                spread(s, k, t)
            along_lat(it, s, k)
        @pl.when(it < STEPS - 1)
        def _():
            state_send(s - 1)

        fill_states(s)
        forward(it, s)
        transport(it, s)
        backward(it)
        return carry

    lax.fori_loop(0, STEPS, step, 0)
    halo_send(STEPS, 1)

    outer_down(STEPS - 1)
    b1d[...] = accd[...].astype(BF16)
    for d in range(1, NX):
        send(b1d.at[:, lax.rem(xx + d, NX)], rxd.at[d - 1], s_x.at[0, d - 1], r_x.at[0], at_x(d))
    outer_up(STEPS - 1)
    b1u[...] = accu[...].astype(BF16)
    for d in range(1, NY):
        send(b1u.at[lax.rem(yy + d, NY)], ryu.at[d - 1], s_y.at[1, d - 1], r_y.at[1], at_y(d))

    taps(0)

    sums = [jnp.sum(kacc[k], axis=0, keepdims=True) for k in range(9)]
    sums.append(jnp.sum(gacc[...], axis=0, keepdims=True))
    table = jnp.concatenate(sums, axis=0)
    for k in range(GROUPS):
        smc[core, 8 * k : 8 * k + 8, :] = table[0:8, 128 * k : 128 * (k + 1)]
        smc[core, 32 + 2 * k : 34 + 2 * k, :] = table[8:10, 128 * k : 128 * (k + 1)]
    send(smc.at[core], smc.at[core], s_sm.at[0], r_sm.at[0], (mate, lat))

    drain(smc.at[0], r_sm.at[0])
    smy[yy] = smc[0] + smc[1]
    for d in range(1, NY):
        send(smy.at[yy], smy.at[yy], s_sm.at[d], r_sm.at[1], at_y(d))

    halo_fill(STEPS, 1)
    for k in range(GROUPS):
        stencil(STEPS, 8, k, 0)
    for i in range(8):
        gs_out[i] = gg[i, 0:16].astype(BF16)

    drain(smy.at[0:3], r_sm.at[1])
    smx[xx] = ((smy[0] + smy[1]) + smy[2]) + smy[3]
    for d in range(1, NX):
        send(smx.at[xx], smx.at[xx], s_sm.at[3 + d], r_sm.at[2], at_x(d))

    drain(rxd, r_x.at[0])
    total = accd[:, xx]
    for d in range(NX - 1):
        total = total + rxd[d].astype(F32)
    b2d[...] = total.astype(BF16)
    for d in range(1, NY):
        send(b2d.at[lax.rem(yy + d, NY)], ryd.at[d - 1], s_y.at[0, d - 1], r_y.at[0], at_y(d))

    drain(ryu, r_y.at[1])
    total = accu[yy]
    for d in range(NY - 1):
        total = total + ryu[d].astype(F32)
    b2u[...] = total.astype(BF16)
    for d in range(1, NX):
        send(b2u.at[lax.rem(xx + d, NX)], rxu.at[d - 1], s_x.at[1, d - 1], r_x.at[1], at_x(d))

    drain(smx.at[0:3], r_sm.at[2])
    here = zl * NZH + zh
    smz[here] = ((smx[0] + smx[1]) + smx[2]) + smx[3]
    for k, (dzl, dzh) in enumerate(zpairs):
        send(smz.at[here], smz.at[here], s_sm.at[7 + k], r_sm.at[3], at_z(dzl, dzh))

    mine = zh * 2 + zl
    alone = zl == core
    for m, r2, own, b3, rz, rsem in (
        (0, ryd, b2d.at[yy], b3d, rzd, r_y.at[0]), (1, rxu, b2u.at[xx], b3u, rzu, r_x.at[1])
    ):
        drain(r2, rsem)
        total = own[...].astype(F32)
        for d in range(3):
            total = total + r2[d].astype(F32)
        b3[...] = total.astype(BF16)
        for k in range(8):
            to_zh, to_core = lax.rem(zh + k // 2, NZH), lax.rem(core + k % 2, 2)
            piece = b3.at[to_zh * 2 + to_core]
            target = ((xx * NZH + to_zh) * 2 + to_core, core * NY + yy)

            def remote(piece=piece, rz=rz, m=m, k=k, target=target):
                send(piece, rz.at[mine], s_z.at[m, k], r_z.at[m], target)

            if k:
                remote()
            else:
                pl.when(jnp.logical_not(alone))(remote)

                @pl.when(alone)
                def _(b3=b3, rz=rz):
                    rz[mine] = b3[zh * 2 + core]

    drain(smz.at[0:7], r_sm.at[3])
    total = smz[0]
    for k in range(1, 8):
        total = total + smz[k]
    for k in range(GROUPS):
        for tap in range(9):
            at_row = 8 * k + tap if tap < 8 else 32 + 2 * k
            kern_out[tap // 3, tap % 3 : tap % 3 + 1, 128 * k : 128 * (k + 1)] = (
                total[at_row : at_row + 1]
            )
        gain_out[:, 128 * k : 128 * (k + 1)] = total[33 + 2 * k : 34 + 2 * k]

    for m, rz, out in ((0, rzd, dn_out), (1, rzu, up_out)):

        @pl.when(alone)
        def _(rz=rz, m=m):
            drain(rz.at[0:7], r_z.at[m])

        @pl.when(jnp.logical_not(alone))
        def _(rz=rz, m=m):
            drain(rz, r_z.at[m])

        total = rz[0].astype(F32)
        for k in range(1, 8):
            total = total + rz[k].astype(F32)
        out[...] = total

    for k in range(len(tables)):
        drain(bt, s_bt.at[k])

    def sent(it, carry):
        for k in range(8):
            drain(st.at[0, 0] if k < 2 else sxs.at[0, 0], s_sx.at[it, k])
        halo_sent(it, WIDE)
        for g in range(GROUPS):
            drain(win.at[it, g, 1 : AHEAD + 1], s_l.at[it, g])
            drain(ps.at[it, g], s_p.at[it, g])
            drain(lw.at[it, g], s_t.at[it, g])
        for k, ref in enumerate((nr, hr, mr, gr)):
            drain(ref.at[it], s_e.at[it, k])
        return carry

    lax.fori_loop(0, STEPS, sent, 0)
    halo_sent(STEPS, 1)
    for m in range(2):
        for k in range(1, 8):
            drain(b3u.at[0], s_z.at[m, k])

        @pl.when(jnp.logical_not(alone))
        def _(m=m):
            drain(b3u.at[0], s_z.at[m, 0])

    for d in range(3):
        drain(rxd.at[0], s_x.at[0, d])
        drain(rxu.at[0], s_x.at[1, d])
        drain(ryd.at[0], s_y.at[0, d])
        drain(ryu.at[0], s_y.at[1, d])
    for k in range(14):
        drain(smc.at[0], s_sm.at[k])


def hand_over(*refs):
    for source, result in zip(refs[:5], refs[5:]):
        result[...] = source[...]


def local(cotangent, states, w_up, w_down, norm_gain, kernel_taps, bilinear, lon_move, lat_move):
    vm, sm = pltpu.VMEM, pltpu.SemaphoreType.DMA
    scratch = [
        vm((8, 16, 512), BF16),
        vm((STEPS, 8, 16, 512), BF16),
        vm((512, 1024), BF16),
        vm((512, 1024), BF16),
        vm((STEPS, 10, PW, 512), F32),
        vm((11, FW, 512), F32),
        vm((9, GW, 512), F32),
        vm((STEPS, 4, WIDE, 8, 16, 128), F32),
        vm((128, 128), F32),
        vm((16, 128), F32),
        vm((2, 16 * WIDE + 16, 128), F32),
        vm((STEPS + 1, 8, 16, 512), BF16),
        vm((STEPS + 1, 16, 512), BF16),
        vm((STEPS + 1, 8, 512), BF16),
        vm((STEPS + 1, 8, 512), BF16),
        vm((STEPS + 1, 3, 8, 512), BF16),
        vm((STEPS + 1, 16, 512), BF16),
        vm((STEPS + 1, 2, 8, 512), BF16),
        vm((STEPS + 1, WIDE, 16, 512), BF16),
        vm((STEPS + 1, WIDE, 2, 16, 512), BF16),
        vm((STEPS, 2, 8, 512), BF16),
        vm((STEPS, 2, 16, 512), BF16),
        vm((STEPS, 6, 8, 512), BF16),
        vm((2 * WIDE + 1, 16, 128), F32),
        vm((STEPS, GROUPS, AHEAD + 1, 8, 16, 128), BF16),
        vm((GROUPS, AHEAD + 1, 8, 16, 128), BF16),
        vm((STEPS, GROUPS, 8, 16, 128), BF16),
        vm((STEPS, GROUPS, 8, 16, 128), BF16),
        vm((GROUPS, 24, 16, 128), BF16),
        vm((STEPS, GROUPS, 2, 8, 16, 128), BF16),
        vm((GROUPS, 8, 48, 128), BF16),
        vm((128, 8 * 48), jnp.int32),
        vm((STEPS, 128, 512), BF16),
        vm((STEPS, 128, 512), BF16),
        vm((STEPS, 128, 512), BF16),
        vm((STEPS, 128, 512), BF16),
        vm((STEPS, 8, 128, 128), BF16),
        vm((STEPS, 4, 128, 128), BF16),
        vm((STEPS, 8, 128, 128), BF16),
        vm((STEPS, 4, 128, 128), BF16),
        vm((8, 128, 128), F32),
        vm((128, 512), F32),
        vm((128, 128), F32),
        vm((128, 512), F32),
        vm((NY, NX, 2 * NZH, 16, 128), F32),
        vm((NY, NX, 2 * NZH, 16, 128), F32),
        vm((9, 8, 512), F32),
        vm((8, 512), F32),
        vm((NY, NX, 2 * NZH, 16, 128), BF16),
        vm((3, NX, 2 * NZH, 16, 128), BF16),
        vm((NX, 2 * NZH, 16, 128), BF16),
        vm((3, 2 * NZH, 16, 128), BF16),
        vm((2 * NZH, 16, 128), BF16),
        vm((8, 16, 128), BF16),
        vm((NY, NX, 2 * NZH, 16, 128), BF16),
        vm((3, NY, 2 * NZH, 16, 128), BF16),
        vm((NY, 2 * NZH, 16, 128), BF16),
        vm((3, 2 * NZH, 16, 128), BF16),
        vm((2 * NZH, 16, 128), BF16),
        vm((8, 16, 128), BF16),
        vm((2, 40, 128), F32),
        vm((NY, 40, 128), F32),
        vm((NX, 40, 128), F32),
        vm((NZL * NZH, 40, 128), F32),
        sm((4,)), sm((STEPS, 8)), sm((STEPS, 2)), sm((7,)), sm,
        sm((STEPS + 1, 3)), sm((STEPS + 1, 3)), sm((STEPS + 1, 3)), sm((STEPS + 1, 3)),
        sm((STEPS + 1, 5)),
        sm((STEPS, GROUPS)), sm((STEPS, GROUPS)),
        sm((STEPS, GROUPS)), sm((STEPS, GROUPS)),
        sm((STEPS, GROUPS)), sm((STEPS, GROUPS)),
        sm((STEPS, 4)), sm((STEPS, 4)),
        sm((2, 3)), sm((2,)), sm((2, 3)), sm((2,)), sm((2, 8)), sm((2,)),
        sm((14,)), sm((4,)),
    ]
    vmem = pl.BlockSpec(memory_space=pltpu.VMEM)
    smem = pl.BlockSpec(memory_space=pltpu.SMEM)
    anywhere = pl.BlockSpec(memory_space=pl.ANY)
    swept = pl.pallas_call(
        kernel,
        out_shape=(
            jax.ShapeDtypeStruct((8, 16, 512), BF16),
            jax.ShapeDtypeStruct((16, 128), F32),
            jax.ShapeDtypeStruct((16, 128), F32),
            jax.ShapeDtypeStruct((3, 3, 512), F32),
            jax.ShapeDtypeStruct((1, 512), F32),
        ),
        in_specs=[anywhere] * 4 + [vmem] * 3 + [smem] * 2,
        out_specs=(vmem,) * 5,
        scratch_shapes=scratch,
        compiler_params=pltpu.CompilerParams(
            collective_id=0, has_side_effects=True, vmem_limit_bytes=56 * 1024 * 1024
        ),
    )(
        cotangent, states, w_up, w_down, norm_gain.reshape(1, 512),
        kernel_taps, bilinear, lon_move, lat_move,
    )
    grad_state, grad_up, grad_down, grad_kernel, grad_gain = pl.pallas_call(
        hand_over,
        out_shape=tuple(jax.ShapeDtypeStruct(a.shape, a.dtype) for a in swept),
        in_specs=[vmem] * 5,
        out_specs=(vmem,) * 5,
    )(*swept)
    return (grad_state, grad_up, grad_down, grad_kernel, grad_gain.reshape(512))


def solution(mesh):
    placed = (
        P("lon", "lat", None),
        P(None, "lon", "lat", None),
        P(),
        P(),
        P(),
        P(),
        P(None, None, "lon", "lat"),
        P(),
        P(),
    )
    return jax.shard_map(
        local,
        mesh=mesh,
        in_specs=placed,
        out_specs=(P("lon", "lat", None), P("lon", "lat"), P("lon", "lat"), P(), P()),
        check_vma=False,
    )
```

```python
import jax
import jax.numpy as jnp
from jax import lax
from jax.experimental import pallas as pl
from jax.experimental.pallas import tpu as pltpu
from jax.sharding import PartitionSpec as P

GROUPS = 4
STEPS = 3
EPSILON = 1e-06
MESH = pl.DeviceIdType.MESH
F32 = jnp.float32
BF16 = jnp.bfloat16

NX, NZH, NZL, NY = 4, 4, 2, 4
LON, LAT = NX * NZH * 2, NZL * NY
AHEAD = 4
PW = 32
FW = 72
WIDE = 3
GW = 24


def kernel(
    cot_hbm, st_hbm, wu_hbm, wd_hbm, gain, kern, bil, lm, lt,
    gs_out, up_out, dn_out, kern_out, gain_out,
    cot, st, wu, wd, px, pf, gg, wb, square, bt, pt, fld, stg, stl, stc, hl, hh, hc, hp, hn, sxs, sxl, sxc, br,
    win, near_by, ps, pr, lon2, lw, lwin, diff,
    mv, mr, nn, nr, hid, hr, gp, gr, ds, nrm, inv, gn, accu, accd, kacc, gacc,
    b1u, ryu, b2u, rxu, b3u, rzu, b1d, rxd, b2d, ryd, b3d, rzd,
    smc, smy, smx, smz,
    s_w, s_sx, r_sx, s_bt, r_bt, s_hl, s_hh, s_hp, s_hn, r_h, s_l, r_l, s_p, r_p, s_t, r_t,
    s_e, r_e, s_y, r_y, s_x, r_x, s_z, r_z, s_sm, r_sm,
):
    lon = lax.axis_index("lon")
    lat = lax.axis_index("lat")
    core = lax.rem(lon, 2)
    chip = lon // 2
    xx, zh = chip // NZH, lax.rem(chip, NZH)
    zl, yy = lat // NY, lax.rem(lat, NY)
    mate = lon + 1 - 2 * core

    def at(dlon, dlat):
        return (lax.rem(lon + dlon + LON, LON), lax.rem(lat + dlat + LAT, LAT))

    def at_y(d):
        return (lon, zl * NY + lax.rem(yy + d, NY))

    def at_x(d):
        return (lax.rem(xx + d, NX) * (2 * NZH) + zh * 2 + core, lat)

    def at_z(dzl, dzh):
        return (
            (xx * NZH + lax.rem(zh + dzh, NZH)) * 2 + core,
            lax.rem(zl + dzl, NZL) * NY + yy,
        )

    def at_pillar(dzl, dzh, dcore):
        return (
            (xx * NZH + lax.rem(zh + dzh, NZH)) * 2 + lax.rem(core + dcore, 2),
            lax.rem(zl + dzl, NZL) * NY + yy,
        )

    def send(src, dst, ssem, rsem, target):
        pltpu.make_async_remote_copy(
            src_ref=src, dst_ref=dst, send_sem=ssem, recv_sem=rsem,
            device_id=target, device_id_type=MESH,
        ).start()

    def drain(ref, sem):
        pltpu.make_async_copy(ref, ref, sem).wait()

    near = [(a, b) for a in (-1, 0, 1) for b in range(-WIDE, WIDE + 1) if (a, b) != (0, 0)]
    zpairs = [(a, b) for a in range(NZL) for b in range(NZH) if (a, b) != (0, 0)]
    pillar = [(a, b, c) for a in range(NZL) for b in range(NZH) for c in range(2) if a + b + c]
    partners = [at(a, b) for a, b in near]
    partners += [at(2 * d * sign, 0) for d in range(1, AHEAD + 1) for sign in (-1, 1)]
    partners += [at_y(d) for d in range(1, NY)] + [at_x(d) for d in range(1, NX)]
    partners += [at_pillar(a, b, c) for a, b, c in pillar]
    barrier = pltpu.get_barrier_semaphore()
    for target in partners:
        pl.semaphore_signal(barrier, inc=1, device_id=target, device_id_type=MESH)

    def column(ref, j):
        return [ref[i, j : j + 1] for i in range(1, 9)]

    def put_column(ref, j, rows):
        for i in range(8):
            ref[i + 1, j : j + 1] = rows[i : i + 1]

    fetch = [
        pltpu.make_async_copy(wu_hbm, wu, s_w.at[0]), pltpu.make_async_copy(wd_hbm, wd, s_w.at[1])
    ]
    first = [
        pltpu.make_async_copy(cot_hbm, cot, s_w.at[2]), pltpu.make_async_copy(st_hbm, st, s_w.at[3])
    ]
    for copy in first + fetch:
        copy.start()

    for copy in first:
        copy.wait()
    not_low = lat > 0
    not_high = lat < LAT - 1
    for i in range(8):
        block = cot[i]
        fld[0, i] = block
        pf[i + 1, 8:24] = block.astype(F32)
        for s in range(STEPS):
            px[s, i + 1, 8:24] = st[s, i].astype(F32)
    for s in range(STEPS):
        for k, j in enumerate((8, 23)):
            sxs[s, k] = jnp.concatenate(column(px.at[s], j), axis=0).astype(BF16)
    square[...] = jnp.zeros_like(square)
    square[0 : 32 * STEPS, 0:16] = bil[...].reshape(32 * STEPS, 16)
    bt[...] = jnp.transpose(square[...])[0:16]
    place = lax.broadcasted_iota(jnp.int32, diff.shape, 0)
    diff[...] = (
        lax.broadcasted_iota(jnp.int32, diff.shape, 1)
        - lax.div(place, 16) * 48 - lax.rem(place, 16)
    )
    pl.semaphore_wait(barrier, len(partners))

    def halo_send(it, tiles):
        first, second, last = column(pf, 8), column(pf, 9), column(pf, 23)
        stg[it] = jnp.concatenate(first + second, axis=0).astype(BF16)
        stl[it] = jnp.concatenate(last, axis=0).astype(BF16)
        corners = [first[7], second[7], first[0], first[1], second[0], second[1]]
        stc[it] = jnp.concatenate(corners + first[0:2], axis=0).astype(BF16)
        for k, a in enumerate((-1, 0, 1)):
            send(stl.at[it], hl.at[it, k], s_hl.at[it, k], r_h.at[it, 0], at(-a, 1))
            if a:
                send(
                    stc.at[it], hc.at[it, k // 2], s_hh.at[it, k], r_h.at[it, 4], at(-a, -tiles)
                )
            else:
                send(stg.at[it], hh.at[it], s_hh.at[it, k], r_h.at[it, 1], at(0, -tiles))
        for t in range(tiles):
            send(fld.at[it, 7], hp.at[it, t], s_hp.at[it, t], r_h.at[it, 2], at(1, -t))
            send(fld.at[it, 0:2], hn.at[it, t], s_hn.at[it, t], r_h.at[it, 3], at(-1, -t))
        if tiles == WIDE:
            for g in range(GROUPS):
                for t in (2, 1):
                    send(
                        fld.at[it, :, :, pl.ds(128 * g, 128)], lw.at[it, g, t - 1],
                        s_t.at[it, g], r_t.at[it, g], at(0, -t),
                    )

    def halo_sent(it, tiles):
        for k in range(3):
            drain(stl.at[it], s_hl.at[it, k])
            drain(stg.at[it] if k == 1 else stc.at[it], s_hh.at[it, k])
        for t in range(tiles):
            drain(fld.at[it, 7], s_hp.at[it, t])
            drain(fld.at[it, 0:2], s_hn.at[it, t])

    def cut(keep, value):
        return jnp.where(keep, value, jnp.zeros_like(value))

    def halo_fill(it, tiles):
        drain(hl.at[it], r_h.at[it, 0])
        drain(hh.at[it], r_h.at[it, 1])
        drain(hc.at[it], r_h.at[it, 4])
        drain(hp.at[it, 0:tiles], r_h.at[it, 2])
        drain(hn.at[it, 0:tiles], r_h.at[it, 3])
        for t in range(tiles):
            inside = lat < LAT - t
            cols = slice(8 + 16 * t, 24 + 16 * t)
            pf[0, cols] = cut(inside, hp[it, t].astype(F32))
            pf[9, cols] = cut(inside, hn[it, t, 0].astype(F32))
            pf[10, cols] = cut(inside, hn[it, t, 1].astype(F32))
        end = 8 + 16 * tiles
        lo = [cut(not_low, hl[it, k].astype(F32)) for k in range(3)]
        hi = cut(lat < LAT - tiles, hh[it].astype(F32))
        before, after = [cut(lat < LAT - tiles, hc[it, k].astype(F32)) for k in range(2)]
        put_column(pf, 7, lo[1])
        put_column(pf, end, hi[0:8])
        put_column(pf, end + 1, hi[8:16])
        pf[0, 7:8] = lo[0][7:8]
        pf[0, end : end + 1] = before[0:1]
        pf[0, end + 1 : end + 2] = before[1:2]
        for r in (0, 1):
            pf[9 + r, 7:8] = lo[2][r : r + 1]
            pf[9 + r, end : end + 1] = after[2 + r : 3 + r]
            pf[9 + r, end + 1 : end + 2] = after[4 + r : 5 + r]

    def tiles_fill(it, g):
        drain(lw.at[it, g], r_t.at[it, g])
        for t in (1, 2):
            for i in range(8):
                pf[i + 1, 8 + 16 * t : 24 + 16 * t, 128 * g : 128 * (g + 1)] = cut(
                    lat < LAT - t, lw[it, g, t - 1, i].astype(F32)
                )

    def stencil(it, rows, k, t):
        on = jnp.where(it > 0, 1.0, 0.0).astype(F32)
        base = 8 + 16 * t
        lanes = pl.ds(128 * k, 128)

        def row(i, carry):
            centre = pf[i + 1, base : base + GW - 2, lanes]
            running = jnp.zeros_like(centre)
            for a in range(3):
                for b in range(3):
                    tap = kern[a, b : b + 1, lanes] * on
                    running = running + tap * (
                        pf[i + 2 - a, base + 1 - b : base + 1 - b + GW - 2, lanes]
                    )
            gg[i, 0 : GW - 2, lanes] = (centre + running).astype(BF16).astype(F32)
            return carry

        lax.fori_loop(0, rows, row, 0, unroll=3 if rows == 9 else 4)

    def exchange(src, dst, it, k):
        send(src, dst.at[it], s_e.at[it, k], r_e.at[it, k], (mate, lat))

    def outer(it, left, left_mate, right, right_mate, acc, first, second):
        drain(left_mate.at[it], r_e.at[it, first])
        drain(right_mate.at[it], r_e.at[it, second])
        tall = jnp.concatenate([left[it], left_mate[it]], axis=0)
        for j in range(2):
            own = [right[it, 4 * core + 2 * j + h] for h in range(2)]
            other = [right_mate[it, 2 * j + h] for h in range(2)]
            wide = jnp.concatenate(
                [jnp.concatenate(own, axis=1), jnp.concatenate(other, axis=1)], axis=0
            )
            part = lax.dot_general(
                tall, wide, (((0,), (0,)), ((), ())), preferred_element_type=F32
            )
            for h in range(2):
                acc[2 * j + h] += part[:, 128 * h : 128 * (h + 1)].reshape(NX, 2 * NZH, 16, 128)

    def outer_down(it):
        outer(it, mv, mr, hid, hr, accd, 2, 1)

    def outer_up(it):
        outer(it, nn, nr, gp, gr, accu, 0, 3)

    def taps(s):
        def row(i, carry):
            f = pf[i + 1, 8:24]
            for a in range(3):
                for b in range(3):
                    prod = px[s, i + a, 7 + b : 23 + b] * f
                    kacc[3 * a + b] += prod[:8] + prod[8:]
            rows = pl.ds(pl.multiple_of(i * 16, 16), 16)
            prod = gn[rows, :] * nrm[rows, :]
            gacc[...] += prod[:8] + prod[8:]
            return carry

        lax.fori_loop(0, 8, row, 0)

    def spread(s, k, t):
        lanes = pl.ds(128 * k, 128)

        def row(i, carry):
            own = wb[s, 0, t, i] * gg[i, 0:16, lanes]
            own = own + wb[s, 1, t, i] * gg[i + 1, 0:16, lanes]
            own = own + wb[s, 2, t, i] * gg[i, 1:17, lanes]
            own = own + wb[s, 3, t, i] * gg[i + 1, 1:17, lanes]
            lwin[k, i, 16 * t : 16 * t + 16] = own.astype(BF16)
            return carry

        lax.fori_loop(0, 8, row, 0, unroll=4)

    def along_lat(it, s, k):
        pick = jnp.where(diff[...] == lt[s, k], 1.0, 0.0).astype(BF16)
        win[it, k, 0] = jnp.dot(
            pick, lwin[k].reshape(8 * 48, 128), preferred_element_type=F32
        ).astype(BF16).reshape(8, 16, 128)
        for d in (2, 1, 3, 4):
            send(
                win.at[it, k, 0], win.at[it, k, d], s_l.at[it, k], r_l.at[it, k],
                at(-2 * d, 0),
            )

    def forward(it, s):
        def row(i, carry):
            u = px[s, i + 1, 8:24]
            running = jnp.zeros_like(u)
            for a in range(3):
                for b in range(3):
                    running = running + kern[a, b : b + 1, :] * (
                        px[s, i + a, 7 + b : 23 + b]
                    )
            u = u + running
            root = lax.rsqrt(jnp.mean(u * u, axis=-1, keepdims=True) + EPSILON)
            rows = pl.ds(pl.multiple_of(i * 16, 16), 16)
            normed = u * root
            nrm[rows, :] = normed
            inv[rows, :] = jnp.broadcast_to(root, (16, 128))
            nn[it, rows, :] = (normed * gain[...]).astype(BF16)
            return carry

        lax.fori_loop(0, 8, row, 0)
        exchange(nn.at[it], nr, it, 0)

        def block(j, carry):
            cols = pl.ds(pl.multiple_of(j * 256, 256), 256)
            pre = jnp.dot(nn[it], wu[:, cols], preferred_element_type=F32)
            sig = jax.nn.sigmoid(pre)
            hidden = (pre * sig).astype(BF16)
            slope = sig * (1.0 + pre * (1.0 - sig))
            for h in range(2):
                hid[it, 2 * j + h] = hidden[:, 128 * h : 128 * (h + 1)]
                ds[2 * j + h] = slope[:, 128 * h : 128 * (h + 1)]
            return carry

        lax.fori_loop(0, 4, block, 0)
        exchange(hid.at[it, pl.ds(4 - 4 * core, 4)], hr, it, 1)

    def transport(it, s):
        def arrive(g):
            drain(win.at[it, g, 1 : AHEAD + 1], r_l.at[it, g])
            for d in range(AHEAD + 1):
                near_by[g, d] = win[it, g, d]
            far = lax.div(lm[s, g], 8)
            ps[it, g] = near_by[g, lax.div(far, 2) + 1 - core]
            send(ps.at[it, g], pr.at[it, g], s_p.at[it, g], r_p.at[it, g], (mate, lat))

        def along(g):
            drain(pr.at[it, g], r_p.at[it, g])
            move = lm[s, g]
            far = lax.div(move, 8)
            odd = pr[it, g]
            lon2[g, 0:8] = odd
            lon2[g, 8:16] = near_by[g, lax.div(far + 1, 2)]
            lon2[g, 16:24] = odd
            begin = 8 - 8 * lax.rem(far, 2) + lax.rem(move, 8)
            for i in range(8):
                mv[it, 16 * i : 16 * i + 16, 128 * g : 128 * (g + 1)] = lon2[g, begin + i]

        for g in range(GROUPS):
            arrive(g)
            along(g)

    def backward(it):
        exchange(mv.at[it], mr, it, 2)
        total = None
        for turn in range(4):
            j = lax.rem(2 - 2 * core + turn, 4)
            cols = pl.ds(pl.multiple_of(j * 256, 256), 256)
            up = jnp.dot(mv[it], wd[:, cols], preferred_element_type=F32)
            slope = jnp.concatenate([ds[2 * j], ds[2 * j + 1]], axis=1)
            pre = (up * slope).astype(BF16)
            gp[it, 2 * j] = pre[:, :128]
            gp[it, 2 * j + 1] = pre[:, 128:]
            if turn == 1:
                exchange(gp.at[it, pl.ds(4 - 4 * core, 4)], gr, it, 3)
            part = lax.dot_general(
                pre, wu[:, cols], (((1,), (1,)), ((), ())), preferred_element_type=F32
            )
            total = part if total is None else total + part
        gn[...] = total

        def row(i, carry):
            rows = pl.ds(pl.multiple_of(i * 16, 16), 16)
            normed = nrm[rows, :]
            scaled = gn[rows, :] * gain[...]
            mean = jnp.mean(scaled * normed, axis=-1, keepdims=True)
            root = jnp.concatenate([inv[rows, :]] * GROUPS, axis=1)
            field = (mv[it, rows, :].astype(F32) + root * (scaled - normed * mean)).astype(BF16)
            fld[it + 1, i] = field
            pf[i + 1, 8:24] = field.astype(F32)
            return carry

        lax.fori_loop(0, 8, row, 0, unroll=True)

    tables = [(a, b) for a in (0, 1) for b in range(WIDE + 1) if a + b]
    for k, (a, b) in enumerate(tables):
        send(bt, br.at[k], s_bt.at[k], r_bt, at(-a, -b))
    halo_send(0, WIDE)

    state_ways = (at(0, 1), at(0, -1), at(1, 1), at(1, -1), at(-1, 1), at(-1, -1))

    def state_send(s):
        for k, (i, target) in enumerate(((7, at(1, 0)), (0, at(-1, 0)))):
            send(st.at[s, i], sxl.at[s, k], s_sx.at[s, k], r_sx.at[s, 0], target)
        for k, target in enumerate(state_ways):
            side = sxs.at[s, 1 - k % 2]
            send(side, sxc.at[s, k], s_sx.at[s, 2 + k], r_sx.at[s, 1], target)

    state_send(STEPS - 1)

    accu[...] = jnp.zeros_like(accu)
    accd[...] = jnp.zeros_like(accd)
    kacc[...] = jnp.zeros_like(kacc)
    gacc[...] = jnp.zeros_like(gacc)

    drain(br, r_bt)
    pt[0, 0:16] = bt[...]
    for k, (a, b) in enumerate(tables):
        pt[a, 16 * b : 16 * b + 16] = cut(lat < LAT - b, br[k])

    def weights(t, carry):
        for i in range(8):
            for q, (di, dj) in enumerate(((0, 0), (1, 0), (0, 1), (1, 1))):
                from_row = pl.multiple_of(t * 16, 16)
                rows = pt[(i + di) // 8, pl.ds(from_row, 24)][dj : dj + 16]
                for s in range(STEPS):
                    lane = (4 * s + q) * 8 + (i + di) % 8
                    wb[s, q, t, i] = jnp.broadcast_to(rows[:, lane : lane + 1], (16, 128))
        return carry

    lax.fori_loop(0, WIDE, weights, 0)

    def fill_states(s):
        drain(sxl.at[s], r_sx.at[s, 0])
        drain(sxc.at[s], r_sx.at[s, 1])
        px[s, 0, 8:24] = sxl[s, 0].astype(F32)
        px[s, 9, 8:24] = sxl[s, 1].astype(F32)
        edge = [
            cut(not_high if k % 2 else not_low, sxc[s, k].astype(F32)) for k in range(6)
        ]
        put_column(px.at[s], 7, edge[0])
        put_column(px.at[s], 24, edge[1])
        px[s, 0, 7:8] = edge[2][7:8]
        px[s, 0, 24:25] = edge[3][7:8]
        px[s, 9, 7:8] = edge[4][0:1]
        px[s, 9, 24:25] = edge[5][0:1]

    for copy in fetch:
        copy.wait()

    def step(it, carry):
        s = STEPS - 1 - it

        @pl.when(it > 0)
        def _():
            halo_send(it, WIDE)
            outer_down(it - 1)
            outer_up(it - 1)
            taps(s + 1)

        halo_fill(it, WIDE)
        for k in range(GROUPS):
            tiles_fill(it, k)
            for t in range(WIDE):
                stencil(it, 9, k, t)
                spread(s, k, t)
            along_lat(it, s, k)
        @pl.when(it < STEPS - 1)
        def _():
            state_send(s - 1)

        fill_states(s)
        forward(it, s)
        transport(it, s)
        backward(it)
        return carry

    lax.fori_loop(0, STEPS, step, 0)
    halo_send(STEPS, 1)

    outer_down(STEPS - 1)
    b1d[...] = accd[...].astype(BF16)
    for d in range(1, NX):
        send(b1d.at[:, lax.rem(xx + d, NX)], rxd.at[d - 1], s_x.at[0, d - 1], r_x.at[0], at_x(d))
    outer_up(STEPS - 1)
    b1u[...] = accu[...].astype(BF16)
    for d in range(1, NY):
        send(b1u.at[lax.rem(yy + d, NY)], ryu.at[d - 1], s_y.at[1, d - 1], r_y.at[1], at_y(d))

    taps(0)

    sums = [jnp.sum(kacc[k], axis=0, keepdims=True) for k in range(9)]
    sums.append(jnp.sum(gacc[...], axis=0, keepdims=True))
    table = jnp.concatenate(sums, axis=0)
    for k in range(GROUPS):
        smc[core, 8 * k : 8 * k + 8, :] = table[0:8, 128 * k : 128 * (k + 1)]
        smc[core, 32 + 2 * k : 34 + 2 * k, :] = table[8:10, 128 * k : 128 * (k + 1)]
    send(smc.at[core], smc.at[core], s_sm.at[0], r_sm.at[0], (mate, lat))

    drain(smc.at[0], r_sm.at[0])
    smy[yy] = smc[0] + smc[1]
    for d in range(1, NY):
        send(smy.at[yy], smy.at[yy], s_sm.at[d], r_sm.at[1], at_y(d))

    halo_fill(STEPS, 1)
    for k in range(GROUPS):
        stencil(STEPS, 8, k, 0)
    for i in range(8):
        gs_out[i] = gg[i, 0:16].astype(BF16)

    drain(smy.at[0:3], r_sm.at[1])
    smx[xx] = ((smy[0] + smy[1]) + smy[2]) + smy[3]
    for d in range(1, NX):
        send(smx.at[xx], smx.at[xx], s_sm.at[3 + d], r_sm.at[2], at_x(d))

    drain(rxd, r_x.at[0])
    total = accd[:, xx]
    for d in range(NX - 1):
        total = total + rxd[d].astype(F32)
    b2d[...] = total.astype(BF16)
    for d in range(1, NY):
        send(b2d.at[lax.rem(yy + d, NY)], ryd.at[d - 1], s_y.at[0, d - 1], r_y.at[0], at_y(d))

    drain(ryu, r_y.at[1])
    total = accu[yy]
    for d in range(NY - 1):
        total = total + ryu[d].astype(F32)
    b2u[...] = total.astype(BF16)
    for d in range(1, NX):
        send(b2u.at[lax.rem(xx + d, NX)], rxu.at[d - 1], s_x.at[1, d - 1], r_x.at[1], at_x(d))

    drain(smx.at[0:3], r_sm.at[2])
    here = zl * NZH + zh
    smz[here] = ((smx[0] + smx[1]) + smx[2]) + smx[3]
    for k, (dzl, dzh) in enumerate(zpairs):
        send(smz.at[here], smz.at[here], s_sm.at[7 + k], r_sm.at[3], at_z(dzl, dzh))

    mine = zh * 2 + zl
    alone = zl == core
    for m, r2, own, b3, rz, rsem in (
        (0, ryd, b2d.at[yy], b3d, rzd, r_y.at[0]), (1, rxu, b2u.at[xx], b3u, rzu, r_x.at[1])
    ):
        drain(r2, rsem)
        total = own[...].astype(F32)
        for d in range(3):
            total = total + r2[d].astype(F32)
        b3[...] = total.astype(BF16)
        for k in range(8):
            to_zh, to_core = lax.rem(zh + k // 2, NZH), lax.rem(core + k % 2, 2)
            piece = b3.at[to_zh * 2 + to_core]
            target = ((xx * NZH + to_zh) * 2 + to_core, core * NY + yy)

            def remote(piece=piece, rz=rz, m=m, k=k, target=target):
                send(piece, rz.at[mine], s_z.at[m, k], r_z.at[m], target)

            if k:
                remote()
            else:
                pl.when(jnp.logical_not(alone))(remote)

                @pl.when(alone)
                def _(b3=b3, rz=rz):
                    rz[mine] = b3[zh * 2 + core]

    drain(smz.at[0:7], r_sm.at[3])
    total = smz[0]
    for k in range(1, 8):
        total = total + smz[k]
    for k in range(GROUPS):
        for tap in range(9):
            at_row = 8 * k + tap if tap < 8 else 32 + 2 * k
            kern_out[tap // 3, tap % 3 : tap % 3 + 1, 128 * k : 128 * (k + 1)] = (
                total[at_row : at_row + 1]
            )
        gain_out[:, 128 * k : 128 * (k + 1)] = total[33 + 2 * k : 34 + 2 * k]

    for m, rz, out in ((0, rzd, dn_out), (1, rzu, up_out)):

        @pl.when(alone)
        def _(rz=rz, m=m):
            drain(rz.at[0:7], r_z.at[m])

        @pl.when(jnp.logical_not(alone))
        def _(rz=rz, m=m):
            drain(rz, r_z.at[m])

        total = rz[0].astype(F32)
        for k in range(1, 8):
            total = total + rz[k].astype(F32)
        out[...] = total

    for k in range(len(tables)):
        drain(bt, s_bt.at[k])

    def sent(it, carry):
        for k in range(8):
            drain(st.at[0, 0] if k < 2 else sxs.at[0, 0], s_sx.at[it, k])
        halo_sent(it, WIDE)
        for g in range(GROUPS):
            drain(win.at[it, g, 1 : AHEAD + 1], s_l.at[it, g])
            drain(ps.at[it, g], s_p.at[it, g])
            drain(lw.at[it, g], s_t.at[it, g])
        for k, ref in enumerate((nr, hr, mr, gr)):
            drain(ref.at[it], s_e.at[it, k])
        return carry

    lax.fori_loop(0, STEPS, sent, 0)
    halo_sent(STEPS, 1)
    for m in range(2):
        for k in range(1, 8):
            drain(b3u.at[0], s_z.at[m, k])

        @pl.when(jnp.logical_not(alone))
        def _(m=m):
            drain(b3u.at[0], s_z.at[m, 0])

    for d in range(3):
        drain(rxd.at[0], s_x.at[0, d])
        drain(rxu.at[0], s_x.at[1, d])
        drain(ryd.at[0], s_y.at[0, d])
        drain(ryu.at[0], s_y.at[1, d])
    for k in range(14):
        drain(smc.at[0], s_sm.at[k])


def hand_over(*refs):
    for source, result in zip(refs[:5], refs[5:]):
        result[...] = source[...]


def local(cotangent, states, w_up, w_down, norm_gain, kernel_taps, bilinear, lon_move, lat_move):
    vm, sm = pltpu.VMEM, pltpu.SemaphoreType.DMA
    scratch = [
        vm((8, 16, 512), BF16),
        vm((STEPS, 8, 16, 512), BF16),
        vm((512, 1024), BF16),
        vm((512, 1024), BF16),
        vm((STEPS, 10, PW, 512), F32),
        vm((11, FW, 512), F32),
        vm((9, GW, 512), F32),
        vm((STEPS, 4, WIDE, 8, 16, 128), F32),
        vm((128, 128), F32),
        vm((16, 128), F32),
        vm((2, 16 * WIDE + 16, 128), F32),
        vm((STEPS + 1, 8, 16, 512), BF16),
        vm((STEPS + 1, 16, 512), BF16),
        vm((STEPS + 1, 8, 512), BF16),
        vm((STEPS + 1, 8, 512), BF16),
        vm((STEPS + 1, 3, 8, 512), BF16),
        vm((STEPS + 1, 16, 512), BF16),
        vm((STEPS + 1, 2, 8, 512), BF16),
        vm((STEPS + 1, WIDE, 16, 512), BF16),
        vm((STEPS + 1, WIDE, 2, 16, 512), BF16),
        vm((STEPS, 2, 8, 512), BF16),
        vm((STEPS, 2, 16, 512), BF16),
        vm((STEPS, 6, 8, 512), BF16),
        vm((2 * WIDE + 1, 16, 128), F32),
        vm((STEPS, GROUPS, AHEAD + 1, 8, 16, 128), BF16),
        vm((GROUPS, AHEAD + 1, 8, 16, 128), BF16),
        vm((STEPS, GROUPS, 8, 16, 128), BF16),
        vm((STEPS, GROUPS, 8, 16, 128), BF16),
        vm((GROUPS, 24, 16, 128), BF16),
        vm((STEPS, GROUPS, 2, 8, 16, 128), BF16),
        vm((GROUPS, 8, 48, 128), BF16),
        vm((128, 8 * 48), jnp.int32),
        vm((STEPS, 128, 512), BF16),
        vm((STEPS, 128, 512), BF16),
        vm((STEPS, 128, 512), BF16),
        vm((STEPS, 128, 512), BF16),
        vm((STEPS, 8, 128, 128), BF16),
        vm((STEPS, 4, 128, 128), BF16),
        vm((STEPS, 8, 128, 128), BF16),
        vm((STEPS, 4, 128, 128), BF16),
        vm((8, 128, 128), F32),
        vm((128, 512), F32),
        vm((128, 128), F32),
        vm((128, 512), F32),
        vm((NY, NX, 2 * NZH, 16, 128), F32),
        vm((NY, NX, 2 * NZH, 16, 128), F32),
        vm((9, 8, 512), F32),
        vm((8, 512), F32),
        vm((NY, NX, 2 * NZH, 16, 128), BF16),
        vm((3, NX, 2 * NZH, 16, 128), BF16),
        vm((NX, 2 * NZH, 16, 128), BF16),
        vm((3, 2 * NZH, 16, 128), BF16),
        vm((2 * NZH, 16, 128), BF16),
        vm((8, 16, 128), BF16),
        vm((NY, NX, 2 * NZH, 16, 128), BF16),
        vm((3, NY, 2 * NZH, 16, 128), BF16),
        vm((NY, 2 * NZH, 16, 128), BF16),
        vm((3, 2 * NZH, 16, 128), BF16),
        vm((2 * NZH, 16, 128), BF16),
        vm((8, 16, 128), BF16),
        vm((2, 40, 128), F32),
        vm((NY, 40, 128), F32),
        vm((NX, 40, 128), F32),
        vm((NZL * NZH, 40, 128), F32),
        sm((4,)), sm((STEPS, 8)), sm((STEPS, 2)), sm((7,)), sm,
        sm((STEPS + 1, 3)), sm((STEPS + 1, 3)), sm((STEPS + 1, 3)), sm((STEPS + 1, 3)),
        sm((STEPS + 1, 5)),
        sm((STEPS, GROUPS)), sm((STEPS, GROUPS)),
        sm((STEPS, GROUPS)), sm((STEPS, GROUPS)),
        sm((STEPS, GROUPS)), sm((STEPS, GROUPS)),
        sm((STEPS, 4)), sm((STEPS, 4)),
        sm((2, 3)), sm((2,)), sm((2, 3)), sm((2,)), sm((2, 8)), sm((2,)),
        sm((14,)), sm((4,)),
    ]
    vmem = pl.BlockSpec(memory_space=pltpu.VMEM)
    smem = pl.BlockSpec(memory_space=pltpu.SMEM)
    anywhere = pl.BlockSpec(memory_space=pl.ANY)
    swept = pl.pallas_call(
        kernel,
        out_shape=(
            jax.ShapeDtypeStruct((8, 16, 512), BF16),
            jax.ShapeDtypeStruct((16, 128), F32),
            jax.ShapeDtypeStruct((16, 128), F32),
            jax.ShapeDtypeStruct((3, 3, 512), F32),
            jax.ShapeDtypeStruct((1, 512), F32),
        ),
        in_specs=[anywhere] * 4 + [vmem] * 3 + [smem] * 2,
        out_specs=(vmem,) * 5,
        scratch_shapes=scratch,
        compiler_params=pltpu.CompilerParams(
            collective_id=0, has_side_effects=True, vmem_limit_bytes=56 * 1024 * 1024
        ),
    )(
        cotangent, states, w_up, w_down, norm_gain.reshape(1, 512),
        kernel_taps, bilinear, lon_move, lat_move,
    )
    grad_state, grad_up, grad_down, grad_kernel, grad_gain = pl.pallas_call(
        hand_over,
        out_shape=tuple(jax.ShapeDtypeStruct(a.shape, a.dtype) for a in swept),
        in_specs=[vmem] * 5,
        out_specs=(vmem,) * 5,
    )(*swept)
    return (grad_state, grad_up, grad_down, grad_kernel, grad_gain.reshape(512))


def solution(mesh):
    placed = (
        P("lon", "lat", None),
        P(None, "lon", "lat", None),
        P(),
        P(),
        P(),
        P(),
        P(None, None, "lon", "lat"),
        P(),
        P(),
    )
    return jax.shard_map(
        local,
        mesh=mesh,
        in_specs=placed,
        out_specs=(P("lon", "lat", None), P("lon", "lat"), P("lon", "lat"), P(), P()),
        check_vma=False,
    )
```
